256 devices in a mesh: row: 8 (over x, core), col: 16 (over y_lo, z), kern: 2 (over y_hi).
Axes of the slice: x: 4, y: 4 (y_hi: 2, y_lo: 2; y = y_hi * 2 + y_lo), z: 8, core: 2. Of those that a mesh axis runs over, the one named last changes fastest.
Arguments:
- mask_levels: int32 [256, 8192], P('row', 'col'), may hold values from 0 to 3
- level_offset: float32 [256, 8192], P('row', 'col'), may hold values from -6 to 6
- target_bits: int32 [256, 8192], P('row', 'col'), may hold values 0 or 1
- socs_kernels: bfloat16 [2, 24, 35, 35], P(None, 'kern'), may hold values from -0.067871094 to 0.067871094
- kernel_weights: float32 [24], P('kern'), may hold values from 0.1 to 1
Outputs:
- resist_image: float32 [256, 8192], P('row', 'col')
- mask_gradient: float32 [256, 8192], P('row', 'col')
The draws below stay inside these ranges and needn't reach their ends.
All inputs are finite; a program needn't handle non-finite values. No bound on the sum of `target_bits` on one device may be relied on, other than what follows from the above.
Results may differ from the reference program's by a relative error of at most 0.0039.
Values may be sent and summed in bfloat16 or wider, within the bound.
No kernel may reach another device: no remote copies, remote signals or barrier semaphores. Data moves between devices by JAX's collectives and lax.ppermute only.
A program may use at most 64 MiB of HBM per device.

```python
import math
import jax
import jax.numpy as jnp
from jax import lax

K = 24
TAPS = 35
NX = 256
NY = 8192


def touch_ends(result, own_key, smallest, largest):
    dims = result.shape
    spot = [jax.random.randint(jax.random.fold_in(own_key, axis), (), 0, dims[axis]) for axis in range(len(dims))]
    result = result.at[tuple(spot)].set(smallest)
    longest = dims.index(max(dims))
    spot[longest] = (spot[longest] + 1) % dims[longest]
    return result.at[tuple(spot)].set(largest)


def levels(stream_key, dims, pieces, least, high):
    def one(axis_at, blocks):
        steps = jax.random.uniform(jax.random.fold_in(jax.random.fold_in(stream_key, 6), axis_at), (blocks,), jnp.float32, least / len(pieces), high / len(pieces))
        return jnp.repeat(jnp.exp(steps), dims[axis_at] // blocks).reshape((-1,) + (1,) * (len(dims) - axis_at - 1))

    level = one(*pieces[0])
    for cut in pieces[1:]:
        level = level * one(*cut)
    return level


def gaussian(rng, extent, width, limit, shards=(), kind=jnp.bfloat16):
    values = jax.random.normal(rng, extent, jnp.float32) * width
    if len(shards) > 0:
        values = levels(rng, extent, shards, -0.22, 0.18) * values
    return jnp.clip(values, min=-limit, max=limit).astype(kind)


def setup_inputs(seed: int = 0) -> dict:
    key_of = jax.random.split(jax.random.key(seed), 6)
    mask_levels = touch_ends(jax.random.randint(key_of[0], (NX, NY), 0, 4), jax.random.fold_in(key_of[0], 1), 0, 3).astype(jnp.int32)
    level_offset = gaussian(key_of[1], (NX, NY), 1.0, 6.0, ((0, 8), (1, 16)), jnp.float32)
    target_bits = touch_ends((jax.random.randint(key_of[2], (NX, NY), 0, 2) < 1).astype(jnp.int32), jax.random.fold_in(key_of[2], 1), 0, 1)
    socs_kernels = gaussian(key_of[3], (2, K, TAPS, TAPS), 0.0112, 0.067871094, ((1, 2),))
    kernel_weights = jnp.clip(jnp.exp(math.log(1.0) - 2.3025851 * jax.random.uniform(key_of[4], (K,), jnp.float32) ** levels(key_of[4], (K,), ((0, 2),), -0.2, 0.2)), 0.1, 1.0)
    return dict(mask_levels=mask_levels, level_offset=level_offset, target_bits=target_bits, socs_kernels=socs_kernels, kernel_weights=kernel_weights)


steepness = 4.0
threshold = 1.0
loss_gain = 32.0


def correlate(field, kernel):
    margin = TAPS // 2
    output = lax.conv_general_dilated(field[None, None], kernel[None, None], (1, 1), ((margin, margin), (margin, margin)), precision=lax.Precision.HIGHEST)
    return output[0, 0]


def reference(mask_levels, level_offset, target_bits, socs_kernels, kernel_weights):
    mask_full = jax.nn.sigmoid(2.0 * (mask_levels.astype(jnp.float32) - 1.5) + level_offset)
    mask_bf = lax.optimization_barrier(mask_full.astype(jnp.bfloat16)).astype(jnp.float32)
    kernels_full = socs_kernels.astype(jnp.float32)
    pairs = (kernels_full[0], kernels_full[1], kernel_weights)

    def intensity_step(running, kernel_pair):
        real_part, imag_part, weight = kernel_pair
        fields_re = correlate(mask_bf, real_part)
        fields_im = correlate(mask_bf, imag_part)
        return running + weight * (fields_re * fields_re + fields_im * fields_im), None

    intensity, _ = lax.scan(intensity_step, jnp.zeros((NX, NY), jnp.float32), pairs)
    resist = jax.nn.sigmoid(steepness * (intensity - threshold))
    slope_term = loss_gain * steepness * (resist - target_bits.astype(jnp.float32)) * resist * (1.0 - resist)

    def gradient_step(running, kernel_pair):
        real_part, imag_part, weight = kernel_pair
        fields_re = correlate(mask_bf, real_part)
        fields_im = correlate(mask_bf, imag_part)
        charge_re = lax.optimization_barrier((2.0 * weight * slope_term * fields_re).astype(jnp.bfloat16)).astype(jnp.float32)
        charge_im = lax.optimization_barrier((2.0 * weight * slope_term * fields_im).astype(jnp.bfloat16)).astype(jnp.float32)
        running = running + correlate(charge_re, real_part[::-1, ::-1]) + correlate(charge_im, imag_part[::-1, ::-1])
        return running, None

    adjoint, _ = lax.scan(gradient_step, jnp.zeros((NX, NY), jnp.float32), pairs)
    return resist, adjoint * mask_full * (1.0 - mask_full)
```

```python
import jax
import jax.numpy as jnp
from jax import lax
from jax.experimental import pallas as pl
from jax.experimental.pallas import tpu as pltpu
from jax.sharding import PartitionSpec as P

STEEP = 4.0
THRESHOLD = 1.0
GAIN = 128.0
TAPS = 35
MARGIN = 17
SLOT = 40
BLOCK = 8
EDGE = 128
ROWS = 32
CHANNELS = 48
REACH = BLOCK + TAPS - 1
FWD_K = 1792
LEAD = 6
WIDE = 384
BF = jnp.bfloat16
F32 = jnp.float32


def body(top, own, bot, tgt, wgt, fwd, adj, res_out, up_out, mid_out, dn_out, rows, image, charge):
    rows[0:32, :] = top[...].astype(F32)
    rows[32:64, :] = own[...].astype(F32)
    rows[64:96, :] = bot[...].astype(F32)
    image[2640:2752, :] = jnp.zeros((112, WIDE), BF)

    def build(p, carry):
        parts = []
        for i in range(2):
            line = jnp.broadcast_to(rows[pl.ds(15 + 2 * p + i, 1), :], (SLOT, 512))
            parts.append(pltpu.roll(line, 0, 1, stride=1, stride_axis=0)[:, 128:])
        both = jnp.concatenate(parts, axis=0).astype(BF)
        image[pl.ds(pl.multiple_of(p * 80, 80), 80), :] = both
        return carry

    lax.fori_loop(0, 33, build, 0)
    weight = wgt[...]
    goal = pltpu.roll(tgt[...].astype(F32), 512 - 111, 1)[:, :WIDE]
    for j in range(4):
        fields = jnp.dot(fwd[...], image[320 * j : 320 * j + FWD_K, :], preferred_element_type=F32)
        fields = fields.reshape(BLOCK, CHANNELS, WIDE)
        intensity = jnp.sum(weight[None] * fields * fields, axis=1)
        resist = jax.nn.sigmoid(STEEP * (intensity - THRESHOLD))
        want = goal[8 * j : 8 * j + 8]
        slope = GAIN * (resist - want) * resist * (1.0 - resist)
        slope = jnp.where(want > 1.5, 0.0, slope)
        scaled = (2.0 * weight)[None] * slope[:, None, :] * fields
        charge[384 * j : 384 * j + 384, :] = scaled.astype(BF).reshape(BLOCK * CHANNELS, WIDE)
        res_out[8 * j : 8 * j + 8, :] = pltpu.roll(resist, WIDE - MARGIN, 1)[:, :256]
    up_out[...] = jnp.zeros((ROWS, 256), F32)
    dn_out[...] = jnp.zeros((ROWS, 256), F32)
    for j in range(9):
        low = max(0, 40 - 8 * j)
        high = min(48, 72 - 8 * j)
        first = low - 40 + 8 * j
        part = jnp.dot(
            adj[:, 48 * low : 48 * high],
            charge[48 * first : 48 * (first + high - low), :],
            preferred_element_type=F32,
        )
        for i in range(BLOCK):
            x = 8 * j + i - MARGIN
            if x > 48:
                continue
            moved = pltpu.roll(part[SLOT * i : SLOT * i + SLOT], 0, 1, stride=1, stride_axis=0)
            line = jnp.sum(moved, axis=0, keepdims=True)
            line = pltpu.roll(line, WIDE - 34, 1)[:, :256]
            if x < 0:
                up_out[ROWS + x : ROWS + x + 1, :] = line
            elif x < ROWS:
                mid_out[x : x + 1, :] = line
            else:
                dn_out[x - ROWS : x - ROWS + 1, :] = line


def per_device(mask_levels, level_offset, target_bits, socs_kernels, kernel_weights):
    kern = lax.axis_index("kern")
    col = lax.axis_index("col")
    n_row, n_col = lax.axis_size("row"), lax.axis_size("col")
    mask_full = jax.nn.sigmoid(2.0 * (mask_levels.astype(F32) - 1.5) + level_offset)
    mask_bf = mask_full.astype(BF)
    target = target_bits.astype(BF)
    left = kern == 0

    strips = jnp.concatenate(
        [
            jnp.where(left, mask_bf[:, :EDGE], mask_bf[:, -EDGE:]),
            jnp.where(left, target[:, :EDGE], target[:, -EDGE:]),
        ],
        axis=0,
    )
    groups = socs_kernels.reshape(8, 3, TAPS, TAPS)
    groups = jnp.pad(groups, ((0, 0), (0, 0), (0, 5), (0, 5)))
    packed = jnp.concatenate([groups[:, 0], groups[:, 1], groups[:, 2]], axis=-1)
    packed = jnp.pad(packed, ((0, 0), (0, 0), (0, 8))).reshape(320, 128)
    high = lax.reduce_precision(kernel_weights, 8, 7)
    middle = lax.reduce_precision(kernel_weights - high, 8, 7)
    lower = kernel_weights - high - middle
    parts = jnp.pad(jnp.stack([high, middle, lower]).astype(BF), ((0, 5), (0, 116)))
    payload = jnp.concatenate([strips, packed, parts], axis=0)
    pairs = []
    for c in range(n_col):
        a, b = (2 * c + 1, 2 * ((c + 1) % n_col))
        pairs += [(a, b), (b, a)]
    other = lax.ppermute(payload, ("col", "kern"), pairs)
    outside = jnp.where(left, col == 0, col == n_col - 1)
    strip_mask = jnp.where(outside, jnp.zeros((), BF), other[:32])
    strip_target = jnp.where(outside, jnp.full((), 2.0, BF), other[32:64])

    def window(value, strip):
        return jnp.where(
            left,
            jnp.concatenate([strip, value[:, :384]], axis=1),
            jnp.concatenate([value[:, 128:], strip], axis=1),
        )

    own = window(mask_bf, strip_mask)
    goal = window(target, strip_target)
    down = [(i, i + 1) for i in range(n_row - 1)]
    upward = [(i + 1, i) for i in range(n_row - 1)]
    top = lax.ppermute(own, "row", down)
    bottom = lax.ppermute(own, "row", upward)

    got = other[64:384].reshape(8, 40, 128)
    got = jnp.stack([got[:, :35, 0:35], got[:, :35, 40:75], got[:, :35, 80:115]], axis=1)
    taps = jnp.concatenate([socs_kernels.reshape(24, TAPS, TAPS), got.reshape(24, TAPS, TAPS)], axis=0)
    far = other[384:387, :12].astype(F32)
    far = (far[0] + far[1]) + far[2]
    weights = jnp.concatenate([kernel_weights, kernel_weights, far, far])
    weights = jnp.broadcast_to(weights[:, None], (CHANNELS, WIDE))
    flat = jnp.pad(taps[:, :, ::-1], ((0, 0), (0, 0), (0, 5))).reshape(CHANNELS, TAPS * SLOT)
    fwd = jnp.concatenate(
        [jnp.pad(flat, ((0, 0), (SLOT * i, FWD_K - 1400 - SLOT * i))) for i in range(BLOCK)], axis=0
    )
    turned = jnp.transpose(taps[:, ::-1, :], (2, 1, 0)).reshape(TAPS, TAPS * CHANNELS)
    turned = jnp.pad(turned, ((0, 5), (0, 0)))
    adj = jnp.concatenate(
        [
            jnp.pad(turned, ((0, 0), (CHANNELS * (LEAD + i), CHANNELS * (48 - TAPS - LEAD - i))))
            for i in range(BLOCK)
        ],
        axis=0,
    )

    tile = jax.ShapeDtypeStruct((ROWS, 256), F32)
    vmem = pl.BlockSpec(memory_space=pltpu.VMEM)
    resist, up, middle_rows, dn = pl.pallas_call(
        body,
        out_shape=(tile,) * 4,
        in_specs=[vmem] * 7,
        out_specs=(vmem,) * 4,
        scratch_shapes=[
            pltpu.VMEM((96, 512), F32),
            pltpu.VMEM((2752, WIDE), BF),
            pltpu.VMEM((1536, WIDE), BF),
        ],
        compiler_params=pltpu.CompilerParams(vmem_limit_bytes=40 * 2**20),
    )(top, own, bottom, goal, weights, fwd, adj)
    from_below = lax.ppermute(up, "row", upward)
    from_above = lax.ppermute(dn, "row", down)
    half = jnp.where(left, mask_full[:, :256], mask_full[:, 256:])
    gradient = (middle_rows + from_below + from_above) * half * (1.0 - half)
    mine = jnp.concatenate([resist, gradient], axis=0)
    theirs = lax.ppermute(mine, "kern", [(0, 1), (1, 0)])
    both = jnp.where(
        left, jnp.concatenate([mine, theirs], axis=1), jnp.concatenate([theirs, mine], axis=1)
    )
    return both[:ROWS], both[ROWS:]


def solution(mesh):
    return jax.shard_map(
        per_device,
        mesh=mesh,
        in_specs=(
            P("row", "col"),
            P("row", "col"),
            P("row", "col"),
            P(None, "kern", None, None),
            P("kern"),
        ),
        out_specs=(P("row", "col"), P("row", "col")),
        check_vma=False,
    )
```

```python
import jax
import jax.numpy as jnp
from jax import lax
from jax.experimental import pallas as pl
from jax.experimental.pallas import tpu as pltpu
from jax.sharding import PartitionSpec as P

STEEP = 4.0
THRESHOLD = 1.0
GAIN = 128.0
TAPS = 35
MARGIN = 17
SLOT = 40
BLOCK = 8
ROWS = 32
CHANNELS = 48
FWD_K = 1792
ADJ_K = 2304
LEAD = 6
WIDE = 384
BF = jnp.bfloat16
F32 = jnp.float32
VMEM = pl.BlockSpec(memory_space=pltpu.VMEM)
HBM = pl.BlockSpec(memory_space=pltpu.HBM)


def start_body(levels, offset, bits, strip, full, short, goal, levels_v, offset_v, bits_v, sems):
    moves = [
        pltpu.make_async_copy(a, b, sems.at[n])
        for n, (a, b) in enumerate([(levels, levels_v), (offset, offset_v), (bits, bits_v)])
    ]
    for move in moves:
        move.start()
    left = lax.axis_index("kern") == 0
    for move in moves:
        move.wait()
    value = jax.nn.sigmoid(2.0 * (levels_v[...].astype(F32) - 1.5) + offset_v[...])
    full[...] = value
    want = bits_v[...].astype(F32)
    short[...] = value.astype(BF)
    goal[...] = want.astype(BF)
    low = lax.broadcasted_iota(jnp.int32, (ROWS, 128), 1) < 64
    ends = jnp.where(low, pltpu.roll(value[:, -128:], 64, 1), want[:, -128:])
    starts = jnp.where(low, value[:, :128], pltpu.roll(want[:, :128], 64, 1))
    strip[...] = jnp.where(left, ends, starts).astype(BF)


def pack_body(kernels, weights, after, packed, padded):
    del after
    padded[...] = jnp.zeros((24, 40, 128), F32)
    row = lax.broadcasted_iota(jnp.int32, (8, 128), 0)
    lane = lax.broadcasted_iota(jnp.int32, (8, 128), 1)
    index = lax.rem(3 * row + jnp.maximum(lane - 120, 0), 12)
    table = jnp.zeros((8, 128), F32)
    for n in range(12):
        table = jnp.where(index == n, weights[n], table)
    table = jnp.where((lane >= 120) & (lane < 123), table, 0.0)
    high = table.astype(BF).astype(F32)
    middle = (table - high).astype(BF).astype(F32)
    lower = table - high - middle
    for n in range(24):
        padded[n, 0:TAPS, 0:TAPS] = kernels[n].astype(F32)
    for g in range(8):
        tile = padded[3 * g]
        tile = tile + pltpu.roll(padded[3 * g + 1], 40, 1)
        tile = tile + pltpu.roll(padded[3 * g + 2], 80, 1)
        extra = jnp.where(
            row == 0, high[g : g + 1], jnp.where(row == 1, middle[g : g + 1], lower[g : g + 1])
        )
        extra = jnp.where(row < 3, extra, 0.0)
        tile = jnp.concatenate([tile[:8] + extra, tile[8:]], axis=0)
        packed[40 * g : 40 * g + 40, :] = tile.astype(BF)


def shifted(tiles, shift, count, lane):
    skip, rest = divmod(shift, 128)
    if rest:
        turned = [None if t is None else pltpu.roll(t, rest, 1) for t in tiles]
    else:
        turned = tiles
    get = lambda n: turned[n] if 0 <= n < len(turned) else None
    out = []
    for n in range(count):
        here = get(n - skip)
        if rest:
            before = get(n - skip - 1)
            if here is not None and before is not None:
                here = jnp.where(lane >= rest, here, before)
            elif here is not None:
                here = jnp.where(lane >= rest, here, 0.0)
            elif before is not None:
                here = jnp.where(lane < rest, before, 0.0)
        out.append(here)
    return out


def taps_body(mine, theirs, fwd, adj, wgt, plain, flipped):
    row = lax.broadcasted_iota(jnp.int32, (128, 128), 0)
    column = lax.broadcasted_iota(jnp.int32, (128, 128), 1)
    group = jnp.where(row >= 80, 2, jnp.where(row >= 40, 1, 0))
    flip = (row + column == 80 * group + 34) & (row < 40 * group + TAPS)
    flip = flip.astype(F32).astype(BF)
    for p, source in enumerate((mine, theirs)):
        block = source[...]
        plain[320 * p : 320 * p + 320, :] = block.astype(F32)
        flipped[320 * p : 320 * p + 320, :] = jnp.dot(block, flip, preferred_element_type=F32)

    def pick(ref, a):
        return jnp.concatenate(
            [ref[pl.ds(a, 8, stride=40), :], ref[pl.ds(320 + a, 8, stride=40), :]], axis=0
        )

    parts = (pick(plain, 0) + pick(plain, 1)) + pick(plain, 2)
    for i in range(3):
        wgt[16 * i : 16 * i + 16, :] = jnp.broadcast_to(parts[:, 120 + i : 121 + i], (16, WIDE))
    lane = lax.broadcasted_iota(jnp.int32, (16, 128), 1)
    empty = jnp.zeros((16, 128), BF)
    for i in range(3):
        tiles = [None] * 11
        for a in range(TAPS):
            first, off = divmod(SLOT * a, 128)
            turned = pick(flipped, a)
            if (off - SLOT * i) % 128:
                turned = pltpu.roll(turned, (off - SLOT * i) % 128, 1)
            inside = min(SLOT, 128 - off)
            piece = jnp.where((lane >= off) & (lane < off + inside), turned, 0.0)
            tiles[first] = piece if tiles[first] is None else tiles[first] + piece
            if inside < SLOT:
                piece = jnp.where(lane < SLOT - inside, turned, 0.0)
                tiles[first + 1] = piece
        for x in range(BLOCK):
            top = 128 * i + 16 * x
            for n, tile in enumerate(shifted(tiles, SLOT * x, 14, lane)):
                fwd[top : top + 16, 128 * n : 128 * n + 128] = (
                    empty if tile is None else tile.astype(BF)
                )
    turned = []
    for q in range(5):
        lines = []
        for e in range(8):
            a = TAPS - 1 - 8 * q - e
            lines.append(pick(plain, a) if a >= 0 else jnp.zeros((16, 128), F32))
        turned.append(jnp.transpose(jnp.concatenate(lines, axis=0)))
    lane = lax.broadcasted_iota(jnp.int32, (SLOT, 128), 1)
    zero = jnp.zeros((SLOT, 128), F32)
    for i in range(3):
        tiles = [t[SLOT * i : SLOT * i + SLOT] for t in turned]
        for x in range(0, BLOCK, 2):
            a = shifted(tiles, 16 * (x + LEAD), 6, lane)
            b = shifted(tiles, 16 * (x + 1 + LEAD), 6, lane)
            for n in range(6):
                both = [zero if t is None else t for t in (a[n], b[n])]
                at = 128 * (3 * n + i)
                adj[SLOT * x : SLOT * (x + 2), at : at + 128] = jnp.concatenate(both, axis=0).astype(BF)


def share(adj, charge, j):
    low = max(0, 40 - 8 * j)
    high = min(48, 72 - 8 * j)
    first = low - 40 + 8 * j
    return jnp.dot(
        adj[:, 48 * low : 48 * high],
        charge[48 * first : 48 * (first + high - low), :],
        preferred_element_type=F32,
    )


def fold(part, i):
    moved = pltpu.roll(part[SLOT * i : SLOT * i + SLOT], 0, 1, stride=1, stride_axis=0)
    line = jnp.sum(moved, axis=0, keepdims=True)
    return pltpu.roll(line, WIDE - 34, 1)[:, :256]


def main_body(one, own, two, tgt, wgt, fwd, adj, res_out, one_out, two_out, some_out, charge, rows, image, up_out, dn_out):
    even = lax.rem(lax.axis_index("row"), 2) == 0
    below = one[...].astype(F32)
    above = two[...].astype(F32)
    rows[0:32, :] = jnp.where(even, above, below)
    rows[32:64, :] = own[...].astype(F32)
    rows[64:96, :] = jnp.where(even, below, above)
    image[2640:2752, :] = jnp.zeros((112, WIDE), BF)
    for p in range(33):
        parts = []
        for i in range(2):
            line = jnp.broadcast_to(rows[15 + 2 * p + i : 16 + 2 * p + i, :], (SLOT, 512))
            parts.append(pltpu.roll(line, 0, 1, stride=1, stride_axis=0)[:, 128:])
        image[80 * p : 80 * p + 80, :] = jnp.concatenate(parts, axis=0).astype(BF)
    weight = wgt[...].reshape(3, 1, 16, WIDE)
    goal = pltpu.roll(tgt[...].astype(F32), 512 - 111, 1)[:, :WIDE]
    for j in range(4):
        fields = jnp.dot(fwd[...], image[320 * j : 320 * j + FWD_K, :], preferred_element_type=F32)
        fields = fields.reshape(3, BLOCK, 16, WIDE)
        squares = weight * fields * fields
        intensity = jnp.sum((squares[0] + squares[1]) + squares[2], axis=1)
        resist = jax.nn.sigmoid(STEEP * (intensity - THRESHOLD))
        want = goal[8 * j : 8 * j + 8]
        slope = GAIN * (resist - want) * resist * (1.0 - resist)
        slope = jnp.where(want > 1.5, 0.0, slope)
        scaled = (2.0 * weight) * slope[None, :, None, :] * fields
        charge[384 * j : 384 * j + 384, :] = scaled.reshape(384, WIDE).astype(BF)
        res_out[8 * j : 8 * j + 8, :] = pltpu.roll(resist, WIDE - MARGIN, 1)[:, :256]
    up_out[0:15, :] = jnp.zeros((15, 256), F32)
    dn_out[17:32, :] = jnp.zeros((15, 256), F32)
    for j in (0, 1, 2, 6, 7, 8):
        part = share(adj, charge, j)
        for i in range(BLOCK):
            x = 8 * j + i - MARGIN
            if x < 0:
                up_out[ROWS + x : ROWS + x + 1, :] = fold(part, i)
            elif ROWS <= x <= ROWS + MARGIN - 1:
                dn_out[x - ROWS : x - ROWS + 1, :] = fold(part, i)
            elif 0 <= x < ROWS:
                some_out[x : x + 1, :] = fold(part, i)
    one_out[...] = jnp.where(even, dn_out[...], up_out[...])
    two_out[...] = jnp.where(even, up_out[...], dn_out[...])


def rest_body(adj, charge, some, mid_out):
    mid_out[0:7, :] = some[0:7, :]
    mid_out[31:32, :] = some[31:32, :]
    for j in (3, 4, 5):
        part = share(adj, charge, j)
        for i in range(BLOCK):
            x = 8 * j + i - MARGIN
            if 0 <= x < ROWS:
                mid_out[x : x + 1, :] = fold(part, i)


def per_device(mask_levels, level_offset, target_bits, socs_kernels, kernel_weights):
    kern = lax.axis_index("kern")
    col = lax.axis_index("col")
    n_row, n_col = lax.axis_size("row"), lax.axis_size("col")
    left = kern == 0
    wide = lambda dtype: jax.ShapeDtypeStruct((ROWS, 512), dtype)
    strip, mask_full, mask_bf, target = pl.pallas_call(
        start_body,
        out_shape=(jax.ShapeDtypeStruct((ROWS, 128), BF), wide(F32), wide(BF), wide(BF)),
        in_specs=[HBM] * 3,
        out_specs=(VMEM,) * 4,
        scratch_shapes=[
            pltpu.VMEM((ROWS, 512), jnp.int32),
            pltpu.VMEM((ROWS, 512), F32),
            pltpu.VMEM((ROWS, 512), jnp.int32),
            pltpu.SemaphoreType.DMA((3,)),
        ],
        compiler_params=pltpu.CompilerParams(vmem_limit_bytes=16 * 2**20),
        name="start",
    )(mask_levels, level_offset, target_bits)
    to_right = [(2 * c, 2 * c + 2) for c in range(n_col - 1)]
    to_left = [(2 * c + 3, 2 * c + 1) for c in range(n_col - 1)]
    strip_in = lax.ppermute(strip, ("col", "kern"), to_right + to_left)
    kernels, _ = lax.optimization_barrier((socs_kernels, strip))
    packed = pl.pallas_call(
        pack_body,
        out_shape=jax.ShapeDtypeStruct((320, 128), BF),
        in_specs=[VMEM, pl.BlockSpec(memory_space=pltpu.SMEM), VMEM],
        out_specs=VMEM,
        scratch_shapes=[pltpu.VMEM((24, 40, 128), F32)],
        compiler_params=pltpu.CompilerParams(vmem_limit_bytes=16 * 2**20),
        cost_estimate=pl.CostEstimate(flops=10**6, bytes_accessed=3 * 10**5, transcendentals=0),
        name="pack",
    )(kernels.reshape(24, TAPS, TAPS), kernel_weights, strip)
    swap = [(0, 1), (1, 0)]
    other = lax.ppermute(packed, "kern", swap)
    outside = jnp.where(left, col == 0, col == n_col - 1)
    edge_mask = jnp.where(outside, jnp.zeros((), BF), strip_in[:, :64])
    edge_target = jnp.where(outside, jnp.full((), 2.0, BF), strip_in[:, 64:])
    blank = jnp.zeros((ROWS, 64), BF)

    def window(value, edge):
        return jnp.where(
            left,
            jnp.concatenate([blank, edge, value[:, :384]], axis=1),
            jnp.concatenate([value[:, 128:], edge, blank], axis=1),
        )

    own = window(mask_bf, edge_mask)
    goal = window(target, edge_target)
    near = [(i, i ^ 1) for i in range(n_row)]
    far = [(i, ((i + 1) ^ 1) - 1) for i in range(1, n_row - 1)]
    one = lax.ppermute(own, "row", near)
    two = lax.ppermute(own, "row", far)
    fwd, adj, weights = pl.pallas_call(
        taps_body,
        out_shape=(
            jax.ShapeDtypeStruct((384, FWD_K), BF),
            jax.ShapeDtypeStruct((SLOT * BLOCK, ADJ_K), BF),
            jax.ShapeDtypeStruct((CHANNELS, WIDE), F32),
        ),
        in_specs=[VMEM] * 2,
        out_specs=(VMEM,) * 3,
        scratch_shapes=[pltpu.VMEM((640, 128), F32), pltpu.VMEM((640, 128), F32)],
        compiler_params=pltpu.CompilerParams(vmem_limit_bytes=16 * 2**20),
        cost_estimate=pl.CostEstimate(flops=4 * 10**8, bytes_accessed=4 * 10**6, transcendentals=0),
        name="taps",
    )(packed, other)
    tile = jax.ShapeDtypeStruct((ROWS, 256), F32)
    resist, share_one, share_two, some, charge = pl.pallas_call(
        main_body,
        out_shape=(tile, tile, tile, tile, jax.ShapeDtypeStruct((1536, WIDE), BF)),
        in_specs=[VMEM] * 7,
        out_specs=(VMEM,) * 5,
        scratch_shapes=[
            pltpu.VMEM((96, 512), F32),
            pltpu.VMEM((2752, WIDE), BF),
            pltpu.VMEM((ROWS, 256), F32),
            pltpu.VMEM((ROWS, 256), F32),
        ],
        compiler_params=pltpu.CompilerParams(vmem_limit_bytes=24 * 2**20),
        cost_estimate=pl.CostEstimate(flops=6 * 10**9, bytes_accessed=6 * 10**6, transcendentals=0),
        name="fields",
    )(one, own, two, goal, weights, fwd, adj)
    got_one = lax.ppermute(share_one, "row", near)
    got_two = lax.ppermute(share_two, "row", far)
    middle_rows = pl.pallas_call(
        rest_body,
        out_shape=tile,
        in_specs=[VMEM] * 3,
        out_specs=VMEM,
        compiler_params=pltpu.CompilerParams(vmem_limit_bytes=16 * 2**20),
        cost_estimate=pl.CostEstimate(flops=2 * 10**9, bytes_accessed=3 * 10**6, transcendentals=0),
        name="inner",
    )(adj, charge, some)
    half = jnp.where(left, mask_full[:, :256], mask_full[:, 256:])
    gradient = (middle_rows + got_one + got_two) * half * (1.0 - half)
    mine = jnp.concatenate([resist, gradient], axis=0)
    theirs = lax.ppermute(mine, "kern", swap)
    both = jnp.where(
        left, jnp.concatenate([mine, theirs], axis=1), jnp.concatenate([theirs, mine], axis=1)
    )
    return both[:ROWS], both[ROWS:]


def solution(mesh):
    return jax.shard_map(
        per_device,
        mesh=mesh,
        in_specs=(
            P("row", "col"),
            P("row", "col"),
            P("row", "col"),
            P(None, "kern", None, None),
            P("kern"),
        ),
        out_specs=(P("row", "col"), P("row", "col")),
        check_vma=False,
    )
```

```python
import jax
import jax.numpy as jnp
from jax import lax
from jax.experimental import pallas as pl
from jax.experimental.pallas import tpu as pltpu
from jax.sharding import PartitionSpec as P

STEEP = 4.0
THRESHOLD = 1.0
GAIN = 128.0
TAPS = 35
MARGIN = 17
SLOT = 40
BLOCK = 8
ROWS = 32
CHANNELS = 48
FWD_K = 1792
ADJ_K = 2304
LEAD = 6
WIDE = 384
START_VMEM = 58 * 2**20
BF = jnp.bfloat16
F32 = jnp.float32
VMEM = pl.BlockSpec(memory_space=pltpu.VMEM)
HBM = pl.BlockSpec(memory_space=pltpu.HBM)


def start_body(levels, offset, bits, kernels, weights, strip, full, short, goal, packed,
               levels_v, offset_v, bits_v, kernels_v, weights_v, lines, sems):
    sources = (kernels, weights, levels, offset, bits)
    targets = (kernels_v, weights_v, levels_v, offset_v, bits_v)
    moves = [pltpu.make_async_copy(a, b, sems.at[n]) for n, (a, b) in enumerate(zip(sources, targets))]
    for move in moves:
        move.start()
    lines[...] = jnp.zeros((840, 128), F32)
    left = lax.axis_index("kern") == 0
    for move in moves[2:]:
        move.wait()
    value = jax.nn.sigmoid(2.0 * (levels_v[...].astype(F32) - 1.5) + offset_v[...])
    full[...] = value
    want = bits_v[...].astype(F32)
    short[...] = value.astype(BF)
    goal[...] = want.astype(BF)
    low = lax.broadcasted_iota(jnp.int32, (ROWS, 128), 1) < 64
    ends = jnp.where(low, pltpu.roll(value[:, -128:], 64, 1), want[:, -128:])
    starts = jnp.where(low, value[:, :128], pltpu.roll(want[:, :128], 64, 1))
    strip[...] = jnp.where(left, ends, starts).astype(BF)
    for move in moves[:2]:
        move.wait()
    for n in range(12):
        lines[70 * n : 70 * n + 70, 0:TAPS] = kernels_v[n].astype(F32).reshape(70, TAPS)
    row = lax.broadcasted_iota(jnp.int32, (8, 128), 0)
    lane = lax.broadcasted_iota(jnp.int32, (8, 128), 1)
    index = 4 * jnp.maximum(lane - 120, 0) + lax.div(row, 2)
    table = jnp.zeros((8, 128), F32)
    for n in range(12):
        table = jnp.where(index == n, weights_v[n], table)
    table = jnp.where((lane >= 120) & (lane < 123), table, 0.0)
    high = table.astype(BF).astype(F32)
    middle = (table - high).astype(BF).astype(F32)
    lower = table - high - middle
    blank = jnp.zeros((SLOT - TAPS, 128), F32)
    for g in range(8):
        at = 70 * (g // 2) + g % 2
        tile = lines[pl.ds(at, TAPS, stride=2), :]
        tile = tile + pltpu.roll(lines[pl.ds(at + 280, TAPS, stride=2), :], 40, 1)
        tile = tile + pltpu.roll(lines[pl.ds(at + 560, TAPS, stride=2), :], 80, 1)
        tile = jnp.concatenate([tile, blank], axis=0)
        extra = jnp.where(
            row == 0, high[g : g + 1], jnp.where(row == 1, middle[g : g + 1], lower[g : g + 1])
        )
        extra = jnp.where(row < 3, extra, 0.0)
        tile = jnp.concatenate([tile[:8] + extra, tile[8:]], axis=0)
        packed[40 * g : 40 * g + 40, :] = tile.astype(BF)


def shifted(tiles, shift, count, lane):
    skip, rest = divmod(shift, 128)
    if rest:
        turned = [None if t is None else pltpu.roll(t, rest, 1) for t in tiles]
    else:
        turned = tiles
    get = lambda n: turned[n] if 0 <= n < len(turned) else None
    out = []
    for n in range(count):
        here = get(n - skip)
        if rest:
            before = get(n - skip - 1)
            if here is not None and before is not None:
                here = jnp.where(lane >= rest, here, before)
            elif here is not None:
                here = jnp.where(lane >= rest, here, 0.0)
            elif before is not None:
                here = jnp.where(lane < rest, before, 0.0)
        out.append(here)
    return out


def taps_body(mine, theirs, fwd, adj, wgt, plain, flipped):
    row = lax.broadcasted_iota(jnp.int32, (128, 128), 0)
    column = lax.broadcasted_iota(jnp.int32, (128, 128), 1)
    group = jnp.where(row >= 80, 2, jnp.where(row >= 40, 1, 0))
    flip = (row + column == 80 * group + 34) & (row < 40 * group + TAPS)
    flip = flip.astype(F32).astype(BF)
    for p, source in enumerate((mine, theirs)):
        block = source[...]
        plain[320 * p : 320 * p + 320, :] = block.astype(F32)
        flipped[320 * p : 320 * p + 320, :] = jnp.dot(block, flip, preferred_element_type=F32)

    def pick(ref, a):
        return jnp.concatenate(
            [ref[pl.ds(a, 8, stride=40), :], ref[pl.ds(320 + a, 8, stride=40), :]], axis=0
        )

    parts = (pick(plain, 0) + pick(plain, 1)) + pick(plain, 2)
    for i in range(3):
        wgt[16 * i : 16 * i + 16, :] = jnp.broadcast_to(parts[:, 120 + i : 121 + i], (16, WIDE))
    lane = lax.broadcasted_iota(jnp.int32, (16, 128), 1)
    empty = jnp.zeros((16, 128), BF)
    for i in range(3):
        tiles = [None] * 11
        for a in range(TAPS):
            first, off = divmod(SLOT * a, 128)
            turned = pick(flipped, a)
            if (off - SLOT * i) % 128:
                turned = pltpu.roll(turned, (off - SLOT * i) % 128, 1)
            inside = min(SLOT, 128 - off)
            piece = jnp.where((lane >= off) & (lane < off + inside), turned, 0.0)
            tiles[first] = piece if tiles[first] is None else tiles[first] + piece
            if inside < SLOT:
                piece = jnp.where(lane < SLOT - inside, turned, 0.0)
                tiles[first + 1] = piece
        for x in range(BLOCK):
            top = 128 * i + 16 * x
            for n, tile in enumerate(shifted(tiles, SLOT * x, 14, lane)):
                fwd[top : top + 16, 128 * n : 128 * n + 128] = (
                    empty if tile is None else tile.astype(BF)
                )
    turned = []
    for q in range(5):
        lines = []
        for e in range(8):
            a = TAPS - 1 - 8 * q - e
            lines.append(pick(plain, a) if a >= 0 else jnp.zeros((16, 128), F32))
        turned.append(jnp.transpose(jnp.concatenate(lines, axis=0)))
    lane = lax.broadcasted_iota(jnp.int32, (SLOT, 128), 1)
    zero = jnp.zeros((SLOT, 128), F32)
    for i in range(3):
        tiles = [t[SLOT * i : SLOT * i + SLOT] for t in turned]
        for x in range(0, BLOCK, 2):
            a = shifted(tiles, 16 * (x + LEAD), 6, lane)
            b = shifted(tiles, 16 * (x + 1 + LEAD), 6, lane)
            for n in range(6):
                both = [zero if t is None else t for t in (a[n], b[n])]
                at = 128 * (3 * n + i)
                adj[SLOT * x : SLOT * (x + 2), at : at + 128] = jnp.concatenate(both, axis=0).astype(BF)


def share(adj, charge, j):
    low = max(0, 40 - 8 * j)
    high = min(48, 72 - 8 * j)
    first = low - 40 + 8 * j
    return jnp.dot(
        adj[:, 48 * low : 48 * high],
        charge[48 * first : 48 * (first + high - low), :],
        preferred_element_type=F32,
    )


def fold(part, i):
    moved = pltpu.roll(part[SLOT * i : SLOT * i + SLOT], 0, 1, stride=1, stride_axis=0)
    line = jnp.sum(moved, axis=0, keepdims=True)
    return pltpu.roll(line, WIDE - 34, 1)[:, :256]


def main_body(one, own, two, tgt, wgt, fwd, adj, res_out, one_out, two_out, some_out, charge, rows, image, up_out, dn_out):
    even = lax.rem(lax.axis_index("row"), 2) == 0
    below = one[...].astype(F32)
    above = two[...].astype(F32)
    rows[0:32, :] = jnp.where(even, above, below)
    rows[32:64, :] = own[...].astype(F32)
    rows[64:96, :] = jnp.where(even, below, above)
    image[2640:2752, :] = jnp.zeros((112, WIDE), BF)
    for p in range(33):
        parts = []
        for i in range(2):
            line = jnp.broadcast_to(rows[15 + 2 * p + i : 16 + 2 * p + i, :], (SLOT, 512))
            parts.append(pltpu.roll(line, 0, 1, stride=1, stride_axis=0)[:, 128:])
        image[80 * p : 80 * p + 80, :] = jnp.concatenate(parts, axis=0).astype(BF)
    weight = wgt[...].reshape(3, 1, 16, WIDE)
    goal = pltpu.roll(tgt[...].astype(F32), 512 - 111, 1)[:, :WIDE]
    for j in range(4):
        fields = jnp.dot(fwd[...], image[320 * j : 320 * j + FWD_K, :], preferred_element_type=F32)
        fields = fields.reshape(3, BLOCK, 16, WIDE)
        squares = weight * fields * fields
        intensity = jnp.sum((squares[0] + squares[1]) + squares[2], axis=1)
        resist = jax.nn.sigmoid(STEEP * (intensity - THRESHOLD))
        want = goal[8 * j : 8 * j + 8]
        slope = GAIN * (resist - want) * resist * (1.0 - resist)
        slope = jnp.where(want > 1.5, 0.0, slope)
        scaled = (2.0 * weight) * slope[None, :, None, :] * fields
        charge[384 * j : 384 * j + 384, :] = scaled.reshape(384, WIDE).astype(BF)
        res_out[8 * j : 8 * j + 8, :] = pltpu.roll(resist, WIDE - MARGIN, 1)[:, :256]
    up_out[0:15, :] = jnp.zeros((15, 256), F32)
    dn_out[17:32, :] = jnp.zeros((15, 256), F32)
    for j in (0, 1, 2, 6, 7, 8):
        part = share(adj, charge, j)
        for i in range(BLOCK):
            x = 8 * j + i - MARGIN
            if x < 0:
                up_out[ROWS + x : ROWS + x + 1, :] = fold(part, i)
            elif ROWS <= x <= ROWS + MARGIN - 1:
                dn_out[x - ROWS : x - ROWS + 1, :] = fold(part, i)
            elif 0 <= x < ROWS:
                some_out[x : x + 1, :] = fold(part, i)
    one_out[...] = jnp.where(even, dn_out[...], up_out[...])
    two_out[...] = jnp.where(even, up_out[...], dn_out[...])


def rest_body(adj, charge, some, mid_out):
    mid_out[0:7, :] = some[0:7, :]
    mid_out[31:32, :] = some[31:32, :]
    for j in (3, 4, 5):
        part = share(adj, charge, j)
        for i in range(BLOCK):
            x = 8 * j + i - MARGIN
            if 0 <= x < ROWS:
                mid_out[x : x + 1, :] = fold(part, i)


def per_device(mask_levels, level_offset, target_bits, socs_kernels, kernel_weights):
    kern = lax.axis_index("kern")
    col = lax.axis_index("col")
    n_row, n_col = lax.axis_size("row"), lax.axis_size("col")
    left = kern == 0
    wide = lambda dtype: jax.ShapeDtypeStruct((ROWS, 512), dtype)
    strip, mask_full, mask_bf, target, packed = pl.pallas_call(
        start_body,
        out_shape=(
            pltpu.VMEM((ROWS, 128), BF),
            pltpu.VMEM((ROWS, 512), F32),
            pltpu.VMEM((ROWS, 512), BF),
            pltpu.VMEM((ROWS, 512), BF),
            pltpu.VMEM((320, 128), BF),
        ),
        in_specs=[HBM] * 5,
        out_specs=(VMEM,) * 5,
        scratch_shapes=[
            pltpu.VMEM((ROWS, 512), jnp.int32),
            pltpu.VMEM((ROWS, 512), F32),
            pltpu.VMEM((ROWS, 512), jnp.int32),
            pltpu.VMEM((12, TAPS, 2, TAPS), BF),
            pltpu.SMEM((12,), F32),
            pltpu.VMEM((840, 128), F32),
            pltpu.SemaphoreType.DMA((5,)),
        ],
        compiler_params=pltpu.CompilerParams(vmem_limit_bytes=START_VMEM),
        name="start",
    )(mask_levels, level_offset, target_bits, jnp.transpose(socs_kernels, (1, 2, 0, 3)), kernel_weights)
    to_right = [(2 * c, 2 * c + 2) for c in range(n_col - 1)]
    to_left = [(2 * c + 3, 2 * c + 1) for c in range(n_col - 1)]
    strip_in = lax.ppermute(strip, ("col", "kern"), to_right + to_left)
    swap = [(0, 1), (1, 0)]
    other = lax.ppermute(packed, "kern", swap)
    outside = jnp.where(left, col == 0, col == n_col - 1)
    edge_mask = jnp.where(outside, jnp.zeros((), BF), strip_in[:, :64])
    edge_target = jnp.where(outside, jnp.full((), 2.0, BF), strip_in[:, 64:])
    blank = jnp.zeros((ROWS, 64), BF)

    def window(value, edge):
        return jnp.where(
            left,
            jnp.concatenate([blank, edge, value[:, :384]], axis=1),
            jnp.concatenate([value[:, 128:], edge, blank], axis=1),
        )

    own = window(mask_bf, edge_mask)
    goal = window(target, edge_target)
    near = [(i, i ^ 1) for i in range(n_row)]
    far = [(i, ((i + 1) ^ 1) - 1) for i in range(1, n_row - 1)]
    one = lax.ppermute(own, "row", near)
    two = lax.ppermute(own, "row", far)
    fwd, adj, weights = pl.pallas_call(
        taps_body,
        out_shape=(
            jax.ShapeDtypeStruct((384, FWD_K), BF),
            jax.ShapeDtypeStruct((SLOT * BLOCK, ADJ_K), BF),
            jax.ShapeDtypeStruct((CHANNELS, WIDE), F32),
        ),
        in_specs=[VMEM] * 2,
        out_specs=(VMEM,) * 3,
        scratch_shapes=[pltpu.VMEM((640, 128), F32), pltpu.VMEM((640, 128), F32)],
        compiler_params=pltpu.CompilerParams(vmem_limit_bytes=16 * 2**20),
        cost_estimate=pl.CostEstimate(flops=4 * 10**8, bytes_accessed=4 * 10**6, transcendentals=0),
        name="taps",
    )(packed, other)
    tile = jax.ShapeDtypeStruct((ROWS, 256), F32)
    resist, share_one, share_two, some, charge = pl.pallas_call(
        main_body,
        out_shape=(tile, tile, tile, tile, jax.ShapeDtypeStruct((1536, WIDE), BF)),
        in_specs=[VMEM] * 7,
        out_specs=(VMEM,) * 5,
        scratch_shapes=[
            pltpu.VMEM((96, 512), F32),
            pltpu.VMEM((2752, WIDE), BF),
            pltpu.VMEM((ROWS, 256), F32),
            pltpu.VMEM((ROWS, 256), F32),
        ],
        compiler_params=pltpu.CompilerParams(vmem_limit_bytes=24 * 2**20),
        cost_estimate=pl.CostEstimate(flops=6 * 10**9, bytes_accessed=6 * 10**6, transcendentals=0),
        name="fields",
    )(one, own, two, goal, weights, fwd, adj)
    got_one = lax.ppermute(share_one, "row", near)
    got_two = lax.ppermute(share_two, "row", far)
    middle_rows = pl.pallas_call(
        rest_body,
        out_shape=tile,
        in_specs=[VMEM] * 3,
        out_specs=VMEM,
        compiler_params=pltpu.CompilerParams(vmem_limit_bytes=16 * 2**20),
        cost_estimate=pl.CostEstimate(flops=2 * 10**9, bytes_accessed=3 * 10**6, transcendentals=0),
        name="inner",
    )(adj, charge, some)
    half = jnp.where(left, mask_full[:, :256], mask_full[:, 256:])
    gradient = (middle_rows + got_one + got_two) * half * (1.0 - half)
    mine = jnp.concatenate([resist, gradient], axis=0)
    mine = lax.reduce_precision(mine, 8, 7)
    theirs = lax.ppermute(mine.astype(BF), "kern", swap).astype(F32)
    both = jnp.where(
        left, jnp.concatenate([mine, theirs], axis=1), jnp.concatenate([theirs, mine], axis=1)
    )
    return both[:ROWS], both[ROWS:]


def solution(mesh):
    return jax.shard_map(
        per_device,
        mesh=mesh,
        in_specs=(
            P("row", "col"),
            P("row", "col"),
            P("row", "col"),
            P(None, "kern", None, None),
            P("kern"),
        ),
        out_specs=(P("row", "col"), P("row", "col")),
        check_vma=False,
    )
```

```python
import jax
import jax.numpy as jnp
from jax import lax
from jax.experimental import pallas as pl
from jax.experimental.pallas import tpu as pltpu
from jax.sharding import PartitionSpec as P

STEEP = 4.0
THRESHOLD = 1.0
GAIN = 128.0
TAPS = 35
MARGIN = 17
SLOT = 40
STEP = 36
BLOCK = 8
ROWS = 32
CHANNELS = 48
FWD_K = 1536
ADJ_K = 2304
LEAD = 6
WIDE = 384
IMAGE = 17 * 4 * STEP
START_VMEM = 58 * 2**20
BF = jnp.bfloat16
F32 = jnp.float32
VMEM = pl.BlockSpec(memory_space=pltpu.VMEM)
HBM = pl.BlockSpec(memory_space=pltpu.HBM)


def start_body(levels, offset, bits, kernels, weights, strip, full, short, goal, packed,
               levels_v, offset_v, bits_v, kernels_v, weights_v, lines, sems):
    sources = (kernels, weights, levels, offset, bits)
    targets = (kernels_v, weights_v, levels_v, offset_v, bits_v)
    moves = [pltpu.make_async_copy(a, b, sems.at[n]) for n, (a, b) in enumerate(zip(sources, targets))]
    for move in moves:
        move.start()
    lines[...] = jnp.zeros((840, 128), F32)
    left = lax.axis_index("kern") == 0
    for move in moves[2:]:
        move.wait()
    value = jax.nn.sigmoid(2.0 * (levels_v[...].astype(F32) - 1.5) + offset_v[...])
    full[...] = value
    want = bits_v[...].astype(F32)
    short[...] = value.astype(BF)
    goal[...] = want.astype(BF)
    low = lax.broadcasted_iota(jnp.int32, (ROWS, 128), 1) < 64
    ends = jnp.where(low, pltpu.roll(value[:, -128:], 64, 1), want[:, -128:])
    starts = jnp.where(low, value[:, :128], pltpu.roll(want[:, :128], 64, 1))
    strip[...] = jnp.where(left, ends, starts).astype(BF)
    for move in moves[:2]:
        move.wait()
    for n in range(12):
        lines[70 * n : 70 * n + 70, 0:TAPS] = kernels_v[n].astype(F32).reshape(70, TAPS)
    row = lax.broadcasted_iota(jnp.int32, (8, 128), 0)
    lane = lax.broadcasted_iota(jnp.int32, (8, 128), 1)
    index = 4 * jnp.maximum(lane - 120, 0) + lax.div(row, 2)
    table = jnp.zeros((8, 128), F32)
    for n in range(12):
        table = jnp.where(index == n, weights_v[n], table)
    table = jnp.where((lane >= 120) & (lane < 123), table, 0.0)
    high = table.astype(BF).astype(F32)
    middle = (table - high).astype(BF).astype(F32)
    lower = table - high - middle
    blank = jnp.zeros((SLOT - TAPS, 128), F32)
    for g in range(8):
        at = 70 * (g // 2) + g % 2
        tile = lines[pl.ds(at, TAPS, stride=2), :]
        tile = tile + pltpu.roll(lines[pl.ds(at + 280, TAPS, stride=2), :], 40, 1)
        tile = tile + pltpu.roll(lines[pl.ds(at + 560, TAPS, stride=2), :], 80, 1)
        tile = jnp.concatenate([tile, blank], axis=0)
        extra = jnp.where(
            row == 0, high[g : g + 1], jnp.where(row == 1, middle[g : g + 1], lower[g : g + 1])
        )
        extra = jnp.where(row < 3, extra, 0.0)
        tile = jnp.concatenate([tile[:8] + extra, tile[8:]], axis=0)
        packed[40 * g : 40 * g + 40, :] = tile.astype(BF)


def shifted(tiles, shift, count, lane):
    skip, rest = divmod(shift, 128)
    if rest:
        turned = [None if t is None else pltpu.roll(t, rest, 1) for t in tiles]
    else:
        turned = tiles
    get = lambda n: turned[n] if 0 <= n < len(turned) else None
    out = []
    for n in range(count):
        here = get(n - skip)
        if rest:
            before = get(n - skip - 1)
            if here is not None and before is not None:
                here = jnp.where(lane >= rest, here, before)
            elif here is not None:
                here = jnp.where(lane >= rest, here, 0.0)
            elif before is not None:
                here = jnp.where(lane < rest, before, 0.0)
        out.append(here)
    return out


def turn(line, count, shift):
    line = jnp.broadcast_to(line, (count, line.shape[1]))
    return pltpu.roll(line, shift, 1, stride=1, stride_axis=0)


def spread(rows, image, first, last):
    early = lax.broadcasted_iota(jnp.int32, (8, 256), 0) < 4
    for n in range(first, last):
        parts = []
        for r in (4 * n, 4 * n + 2):
            a, b = rows[r : r + 1, :WIDE], rows[r + 1 : r + 2, :WIDE]
            parts.append(turn(a, 32, 0)[:, 128:])
            mixed = pltpu.roll(turn(b, 8, 0)[:, 128:], 4, 0)
            parts.append(jnp.where(early, turn(a, 8, 32)[:, 128:], mixed))
            parts.append(turn(b, 32, 4)[:, 128:])
        image[144 * n : 144 * n + 144, :] = jnp.concatenate(parts, axis=0).astype(BF)


def spread_ends(rows, side, lines, ends):
    low = lax.broadcasted_iota(jnp.int32, (24, 128), 1) < 64
    side[...] = pltpu.roll(rows[:, 256:], 192, 1)[:, :128]
    for e in range(2):
        moved = [side[pl.ds(8 * j + e, 24, stride=2), :] for j in range(4)]
        for n in range(5):
            shift = 8 * n - 4 * e
            for t in range(2):
                one = pltpu.roll(moved[2 * t], (shift - 56) % 128, 1)
                two = pltpu.roll(moved[2 * t + 1], (shift + 8) % 128, 1)
                at = 24 * (5 * e + n)
                lines[at : at + 24, 128 * t : 128 * t + 128] = jnp.where(low, one, two)
    early = lax.broadcasted_iota(jnp.int32, (8, 128), 0) < 4
    for t in range(2):
        lanes = slice(128 * t, 128 * t + 128)
        parts = []
        for c in range(21):
            get = lambda e, n: turn(lines[24 * (5 * e + n) + c : 24 * (5 * e + n) + c + 1, lanes], 8, 0)
            parts += [get(0, n) for n in range(4)]
            parts.append(jnp.where(early, get(0, 4), get(1, 0)))
            parts += [get(1, n) for n in range(1, 5)]
            if c % 2:
                ends[72 * (c - 1) : 72 * (c + 1), lanes] = jnp.concatenate(parts, axis=0).astype(BF)
                parts = []
        parts.append(jnp.zeros((24, 128), F32))
        ends[1440:1536, lanes] = jnp.concatenate(parts, axis=0).astype(BF)


def taps_body(mine, theirs, own, fwd, adj, wgt, image, plain, flipped, rows):
    rows[17:49, :] = own[...].astype(F32)
    spread(rows, image, 5, 12)
    row = lax.broadcasted_iota(jnp.int32, (128, 128), 0)
    column = lax.broadcasted_iota(jnp.int32, (128, 128), 1)
    group = jnp.where(row >= 80, 2, jnp.where(row >= 40, 1, 0))
    flip = (row + column == 80 * group + 34) & (row < 40 * group + TAPS)
    flip = flip.astype(F32).astype(BF)
    for p, source in enumerate((mine, theirs)):
        block = source[...]
        plain[320 * p : 320 * p + 320, :] = block.astype(F32)
        flipped[320 * p : 320 * p + 320, :] = jnp.dot(block, flip, preferred_element_type=F32)

    def pick(ref, a):
        return jnp.concatenate(
            [ref[pl.ds(a, 8, stride=40), :], ref[pl.ds(320 + a, 8, stride=40), :]], axis=0
        )

    parts = (pick(plain, 0) + pick(plain, 1)) + pick(plain, 2)
    for i in range(3):
        wgt[16 * i : 16 * i + 16, :] = jnp.broadcast_to(parts[:, 120 + i : 121 + i], (16, 256))
    lane = lax.broadcasted_iota(jnp.int32, (16, 128), 1)
    empty = jnp.zeros((16, 128), BF)
    for i in range(3):
        tiles = [None] * 10
        for a in range(TAPS):
            first, off = divmod(STEP * a, 128)
            turned = pick(flipped, a)
            if (off - SLOT * i) % 128:
                turned = pltpu.roll(turned, (off - SLOT * i) % 128, 1)
            inside = min(STEP, 128 - off)
            piece = jnp.where((lane >= off) & (lane < off + inside), turned, 0.0)
            tiles[first] = piece if tiles[first] is None else tiles[first] + piece
            if inside < STEP:
                piece = jnp.where(lane < STEP - inside, turned, 0.0)
                tiles[first + 1] = piece
        for x in range(BLOCK):
            top = 128 * i + 16 * x
            for n, tile in enumerate(shifted(tiles, STEP * x, 12, lane)):
                fwd[top : top + 16, 128 * n : 128 * n + 128] = (
                    empty if tile is None else tile.astype(BF)
                )
    turned = []
    for q in range(5):
        lines = []
        for e in range(8):
            a = TAPS - 1 - 8 * q - e
            lines.append(pick(plain, a) if a >= 0 else jnp.zeros((16, 128), F32))
        turned.append(jnp.transpose(jnp.concatenate(lines, axis=0)))
    lane = lax.broadcasted_iota(jnp.int32, (SLOT, 128), 1)
    zero = jnp.zeros((SLOT, 128), F32)
    for i in range(3):
        tiles = [t[SLOT * i : SLOT * i + SLOT] for t in turned]
        for x in range(0, BLOCK, 2):
            a = shifted(tiles, 16 * (x + LEAD), 6, lane)
            b = shifted(tiles, 16 * (x + 1 + LEAD), 6, lane)
            for n in range(6):
                both = [zero if t is None else t for t in (a[n], b[n])]
                at = 128 * (3 * n + i)
                adj[SLOT * x : SLOT * (x + 2), at : at + 128] = jnp.concatenate(both, axis=0).astype(BF)


def share(adj, charge, j, count=BLOCK):
    low = max(0, 40 - 8 * j)
    high = min(48, 72 - 8 * j)
    first = low - 40 + 8 * j
    return jnp.dot(
        adj[: SLOT * count, 48 * low : 48 * high],
        charge[48 * first : 48 * (first + high - low), :],
        preferred_element_type=F32,
    )


def fold(part, i):
    moved = pltpu.roll(part[SLOT * i : SLOT * i + SLOT], 0, 1, stride=1, stride_axis=0)
    line = jnp.sum(moved, axis=0, keepdims=True)
    return pltpu.roll(line, WIDE - 34, 1)[:, :256]


def main_body(one, own, two, tgt, wgt, fwd, adj, image_in, res_out, one_out, two_out, some_out, charge,
              image, rows, side, lines, ends, up_out, dn_out):
    del image_in
    even = lax.rem(lax.axis_index("row"), 2) == 0
    below = one[...].astype(F32)
    above = two[...].astype(F32)
    rows[0:17, :] = jnp.where(even, above, below)[15:32]
    rows[17:49, :] = own[...].astype(F32)
    rows[49:66, :] = jnp.where(even, below, above)[0:17]
    rows[66:72, :] = jnp.zeros((6, 512), F32)
    spread(rows, image, 0, 5)
    spread(rows, image, 12, 17)
    spread_ends(rows, side, lines, ends)
    weight = wgt[...].reshape(3, 1, 16, 256)
    target = tgt[...].astype(F32)
    goal = pltpu.roll(target, 512 - 111, 1)[:, :256]
    low = lax.broadcasted_iota(jnp.int32, (8, 128), 1) < 64
    late = lax.broadcasted_iota(jnp.int32, (8, 128), 1) >= 111

    def tail(j):
        return pltpu.roll(target[8 * j : 8 * j + 8, 256:], (64 * (j % 2) - 103) % 256, 1)[:, :128]

    goal_ends = [jnp.where(low, tail(0), tail(1)), jnp.where(low, tail(2), tail(3))]

    def respond(pixels, want):
        fields = jnp.dot(fwd[...], pixels, preferred_element_type=F32)
        fields = fields.reshape(3, BLOCK, 16, 256)
        squares = weight * fields * fields
        intensity = jnp.sum((squares[0] + squares[1]) + squares[2], axis=1)
        resist = jax.nn.sigmoid(STEEP * (intensity - THRESHOLD))
        slope = GAIN * (resist - want) * resist * (1.0 - resist)
        slope = jnp.where(want > 1.5, 0.0, slope)
        scaled = (2.0 * weight) * slope[None, :, None, :] * fields
        return resist, scaled.reshape(384, 256)

    resist_ends, scaled = respond(ends[...], jnp.concatenate(goal_ends, axis=1))
    for j in range(4):
        tile = scaled[:, 128 * (j // 2) : 128 * (j // 2) + 128]
        tile = pltpu.roll(tile, 120 - 64 * (j % 2), 1)
        charge[384 * j : 384 * j + 384, 256:] = tile.astype(BF)
    for j in range(4):
        resist, scaled = respond(image[288 * j : 288 * j + FWD_K, :], goal[8 * j : 8 * j + 8])
        charge[384 * j : 384 * j + 384, :256] = scaled.astype(BF)
        resist = pltpu.roll(resist, 256 - MARGIN, 1)
        end = resist_ends[:, 128 * (j // 2) : 128 * (j // 2) + 128]
        end = pltpu.roll(end, (103 - 64 * (j % 2)) % 128, 1)
        res_out[8 * j : 8 * j + 8, :128] = resist[:, :128]
        res_out[8 * j : 8 * j + 8, 128:] = jnp.where(late, end, resist[:, 128:])
    up_out[0:15, :] = jnp.zeros((15, 256), F32)
    dn_out[17:32, :] = jnp.zeros((15, 256), F32)
    for j, count in ((0, 8), (1, 8), (2, 1), (6, 8), (7, 8), (8, 2)):
        part = share(adj, charge, j, count)
        for i in range(count):
            x = 8 * j + i - MARGIN
            if x < 0:
                up_out[ROWS + x : ROWS + x + 1, :] = fold(part, i)
            elif x < ROWS:
                some_out[...] = jnp.broadcast_to(fold(part, i), (8, 256))
            else:
                dn_out[x - ROWS : x - ROWS + 1, :] = fold(part, i)
    one_out[...] = jnp.where(even, dn_out[...], up_out[...])
    two_out[...] = jnp.where(even, up_out[...], dn_out[...])


def rest_body(adj, charge, some, mid_out):
    mid_out[31:32, :] = some[0:1, :]
    for j in (2, 3, 4, 5):
        part = share(adj, charge, j)
        for i in range(BLOCK):
            x = 8 * j + i - MARGIN
            if x >= 0:
                mid_out[x : x + 1, :] = fold(part, i)


def per_device(mask_levels, level_offset, target_bits, socs_kernels, kernel_weights):
    kern = lax.axis_index("kern")
    col = lax.axis_index("col")
    n_row, n_col = lax.axis_size("row"), lax.axis_size("col")
    left = kern == 0
    wide = lambda dtype: jax.ShapeDtypeStruct((ROWS, 512), dtype)
    strip, mask_full, mask_bf, target, packed = pl.pallas_call(
        start_body,
        out_shape=(
            pltpu.VMEM((ROWS, 128), BF),
            pltpu.VMEM((ROWS, 512), F32),
            pltpu.VMEM((ROWS, 512), BF),
            pltpu.VMEM((ROWS, 512), BF),
            pltpu.VMEM((320, 128), BF),
        ),
        in_specs=[HBM] * 5,
        out_specs=(VMEM,) * 5,
        scratch_shapes=[
            pltpu.VMEM((ROWS, 512), jnp.int32),
            pltpu.VMEM((ROWS, 512), F32),
            pltpu.VMEM((ROWS, 512), jnp.int32),
            pltpu.VMEM((12, TAPS, 2, TAPS), BF),
            pltpu.SMEM((12,), F32),
            pltpu.VMEM((840, 128), F32),
            pltpu.SemaphoreType.DMA((5,)),
        ],
        compiler_params=pltpu.CompilerParams(vmem_limit_bytes=START_VMEM),
        name="start",
    )(mask_levels, level_offset, target_bits, jnp.transpose(socs_kernels, (1, 2, 0, 3)), kernel_weights)
    to_right = [(2 * c, 2 * c + 2) for c in range(n_col - 1)]
    to_left = [(2 * c + 3, 2 * c + 1) for c in range(n_col - 1)]
    strip_in = lax.ppermute(strip, ("col", "kern"), to_right + to_left)
    swap = [(0, 1), (1, 0)]
    other = lax.ppermute(packed, "kern", swap)
    outside = jnp.where(left, col == 0, col == n_col - 1)
    edge_mask = jnp.where(outside, jnp.zeros((), BF), strip_in[:, :64])
    edge_target = jnp.where(outside, jnp.full((), 2.0, BF), strip_in[:, 64:])
    blank = jnp.zeros((ROWS, 64), BF)

    def window(value, edge):
        return jnp.where(
            left,
            jnp.concatenate([blank, edge, value[:, :384]], axis=1),
            jnp.concatenate([value[:, 128:], edge, blank], axis=1),
        )

    own = window(mask_bf, edge_mask)
    goal = window(target, edge_target)
    near = [(i, i ^ 1) for i in range(n_row)]
    far = [(i, ((i + 1) ^ 1) - 1) for i in range(1, n_row - 1)]
    one = lax.ppermute(own, "row", near)
    two = lax.ppermute(own, "row", far)
    fwd, adj, weights, image = pl.pallas_call(
        taps_body,
        out_shape=(
            jax.ShapeDtypeStruct((384, FWD_K), BF),
            jax.ShapeDtypeStruct((SLOT * BLOCK, ADJ_K), BF),
            jax.ShapeDtypeStruct((CHANNELS, 256), F32),
            jax.ShapeDtypeStruct((IMAGE, 256), BF),
        ),
        in_specs=[VMEM] * 3,
        out_specs=(VMEM,) * 4,
        scratch_shapes=[
            pltpu.VMEM((640, 128), F32),
            pltpu.VMEM((640, 128), F32),
            pltpu.VMEM((56, 512), F32),
        ],
        compiler_params=pltpu.CompilerParams(vmem_limit_bytes=16 * 2**20),
        cost_estimate=pl.CostEstimate(flops=4 * 10**8, bytes_accessed=4 * 10**6, transcendentals=0),
        name="taps",
    )(packed, other, own)
    tile = jax.ShapeDtypeStruct((ROWS, 256), F32)
    resist, share_one, share_two, some, charge, _ = pl.pallas_call(
        main_body,
        out_shape=(
            tile,
            tile,
            tile,
            jax.ShapeDtypeStruct((8, 256), F32),
            jax.ShapeDtypeStruct((1536, WIDE), BF),
            jax.ShapeDtypeStruct((IMAGE, 256), BF),
        ),
        input_output_aliases={7: 5},
        in_specs=[VMEM] * 8,
        out_specs=(VMEM,) * 6,
        scratch_shapes=[
            pltpu.VMEM((72, 512), F32),
            pltpu.VMEM((72, 128), F32),
            pltpu.VMEM((240, 256), F32),
            pltpu.VMEM((FWD_K, 256), BF),
            pltpu.VMEM((ROWS, 256), F32),
            pltpu.VMEM((ROWS, 256), F32),
        ],
        compiler_params=pltpu.CompilerParams(vmem_limit_bytes=24 * 2**20),
        cost_estimate=pl.CostEstimate(flops=6 * 10**9, bytes_accessed=6 * 10**6, transcendentals=0),
        name="fields",
    )(one, own, two, goal, weights, fwd, adj, image)
    got_one = lax.ppermute(share_one, "row", near)
    got_two = lax.ppermute(share_two, "row", far)
    middle_rows = pl.pallas_call(
        rest_body,
        out_shape=tile,
        in_specs=[VMEM] * 3,
        out_specs=VMEM,
        compiler_params=pltpu.CompilerParams(vmem_limit_bytes=16 * 2**20),
        cost_estimate=pl.CostEstimate(flops=2 * 10**9, bytes_accessed=3 * 10**6, transcendentals=0),
        name="inner",
    )(adj, charge, some)
    half = jnp.where(left, mask_full[:, :256], mask_full[:, 256:])
    gradient = (middle_rows + got_one + got_two) * half * (1.0 - half)
    mine = jnp.concatenate([resist, gradient], axis=0)
    mine = lax.reduce_precision(mine, 8, 7)
    theirs = lax.ppermute(mine.astype(BF), "kern", swap).astype(F32)
    both = jnp.where(
        left, jnp.concatenate([mine, theirs], axis=1), jnp.concatenate([theirs, mine], axis=1)
    )
    return both[:ROWS], both[ROWS:]


def solution(mesh):
    return jax.shard_map(
        per_device,
        mesh=mesh,
        in_specs=(
            P("row", "col"),
            P("row", "col"),
            P("row", "col"),
            P(None, "kern", None, None),
            P("kern"),
        ),
        out_specs=(P("row", "col"), P("row", "col")),
        check_vma=False,
    )
```

```python
import jax
import jax.numpy as jnp
from jax import lax
from jax.experimental import pallas as pl
from jax.experimental.pallas import tpu as pltpu
from jax.sharding import PartitionSpec as P

STEEP = 4.0
THRESHOLD = 1.0
GAIN = 128.0
TAPS = 35
MARGIN = 17
SLOT = 40
STEP = 36
BLOCK = 8
ROWS = 32
CHANNELS = 48
FWD_K = 1536
ADJ_K = 2304
LEAD = 6
WIDE = 384
IMAGE = 17 * 4 * STEP
START_VMEM = 58 * 2**20
BF = jnp.bfloat16
F32 = jnp.float32
VMEM = pl.BlockSpec(memory_space=pltpu.VMEM)
HBM = pl.BlockSpec(memory_space=pltpu.HBM)


def start_body(levels, offset, bits, kernels, weights, strip, full, short, goal, kernels_v, parts,
               levels_v, offset_v, bits_v, weights_v, sems):
    sources = (kernels, weights, levels, offset, bits)
    targets = (kernels_v, weights_v, levels_v, offset_v, bits_v)
    moves = [pltpu.make_async_copy(a, b, sems.at[n]) for n, (a, b) in enumerate(zip(sources, targets))]
    for move in moves:
        move.start()
    left = lax.axis_index("kern") == 0
    for move in moves[2:]:
        move.wait()
    value = jax.nn.sigmoid(2.0 * (levels_v[...].astype(F32) - 1.5) + offset_v[...])
    full[...] = value
    want = bits_v[...].astype(F32)
    short[...] = value.astype(BF)
    goal[...] = want.astype(BF)
    low = lax.broadcasted_iota(jnp.int32, (ROWS, 128), 1) < 64
    ends = jnp.where(low, pltpu.roll(value[:, -128:], 64, 1), want[:, -128:])
    starts = jnp.where(low, value[:, :128], pltpu.roll(want[:, :128], 64, 1))
    strip[...] = jnp.where(left, ends, starts).astype(BF)
    for move in moves[:2]:
        move.wait()
    row = lax.broadcasted_iota(jnp.int32, (8, 128), 0)
    lane = lax.broadcasted_iota(jnp.int32, (8, 128), 1)
    index = 4 * jnp.maximum(lane - 120, 0) + lax.rem(row, 4)
    table = jnp.zeros((8, 128), F32)
    for n in range(12):
        table = jnp.where(index == n, weights_v[n], table)
    table = jnp.where((lane >= 120) & (lane < 123), table, 0.0)
    high = table.astype(BF).astype(F32)
    middle = (table - high).astype(BF).astype(F32)
    lower = table - high - middle
    parts[0:8, :] = high
    parts[8:16, :] = middle
    parts[16:24, :] = lower


def pack_body(kernels, parts, packed, plane, lines):
    plane[...] = jnp.zeros((72, 128), F32)
    for n in range(12):
        plane[0:70, 0:TAPS] = kernels[n].astype(F32).reshape(70, TAPS)
        lines[pl.ds(280 * (n // 4) + n % 4, 70, stride=4), :] = plane[0:70, :]
    lines[0:24, :] = lines[0:24, :] + parts[...]
    tile = lines[0:280, :] + pltpu.roll(lines[280:560, :], 40, 1) + pltpu.roll(lines[560:840, :], 80, 1)
    packed[...] = tile.astype(BF)


def shifted(tiles, shift, count, lane):
    skip, rest = divmod(shift, 128)
    if rest:
        turned = [None if t is None else pltpu.roll(t, rest, 1) for t in tiles]
    else:
        turned = tiles
    get = lambda n: turned[n] if 0 <= n < len(turned) else None
    out = []
    for n in range(count):
        here = get(n - skip)
        if rest:
            before = get(n - skip - 1)
            if here is not None and before is not None:
                here = jnp.where(lane >= rest, here, before)
            elif here is not None:
                here = jnp.where(lane >= rest, here, 0.0)
            elif before is not None:
                here = jnp.where(lane < rest, before, 0.0)
        out.append(here)
    return out


def turn(line, count, shift):
    line = jnp.broadcast_to(line, (count, line.shape[1]))
    return pltpu.roll(line, shift, 1, stride=1, stride_axis=0)


def spread(rows, image, first, last):
    early = lax.broadcasted_iota(jnp.int32, (8, 256), 0) < 4
    for n in range(first, last):
        parts = []
        for r in (4 * n, 4 * n + 2):
            a, b = rows[r : r + 1, :WIDE], rows[r + 1 : r + 2, :WIDE]
            parts.append(turn(a, 32, 0)[:, 128:])
            mixed = pltpu.roll(turn(b, 8, 0)[:, 128:], 4, 0)
            parts.append(jnp.where(early, turn(a, 8, 32)[:, 128:], mixed))
            parts.append(turn(b, 32, 4)[:, 128:])
        image[144 * n : 144 * n + 144, :] = jnp.concatenate(parts, axis=0).astype(BF)


def spread_ends(rows, side, lines, ends):
    low = lax.broadcasted_iota(jnp.int32, (24, 128), 1) < 64
    side[...] = pltpu.roll(rows[:, 256:], 192, 1)[:, :128]
    for e in range(2):
        moved = [side[pl.ds(8 * j + e, 24, stride=2), :] for j in range(4)]
        for n in range(5):
            shift = 8 * n - 4 * e
            for t in range(2):
                one = pltpu.roll(moved[2 * t], (shift - 56) % 128, 1)
                two = pltpu.roll(moved[2 * t + 1], (shift + 8) % 128, 1)
                at = 24 * (5 * e + n)
                lines[at : at + 24, 128 * t : 128 * t + 128] = jnp.where(low, one, two)
    early = lax.broadcasted_iota(jnp.int32, (8, 128), 0) < 4
    for t in range(2):
        lanes = slice(128 * t, 128 * t + 128)
        parts = []
        for c in range(21):
            get = lambda e, n: turn(lines[24 * (5 * e + n) + c : 24 * (5 * e + n) + c + 1, lanes], 8, 0)
            parts += [get(0, n) for n in range(4)]
            parts.append(jnp.where(early, get(0, 4), get(1, 0)))
            parts += [get(1, n) for n in range(1, 5)]
            if c % 2:
                ends[72 * (c - 1) : 72 * (c + 1), lanes] = jnp.concatenate(parts, axis=0).astype(BF)
                parts = []
        parts.append(jnp.zeros((24, 128), F32))
        ends[1440:1536, lanes] = jnp.concatenate(parts, axis=0).astype(BF)


def own_body(own, image, rows):
    rows[17:49, :] = own[...].astype(F32)
    spread(rows, image, 5, 12)


def taps_body(mine, theirs, fwd, adj, wgt, plain, flipped):
    row = lax.broadcasted_iota(jnp.int32, (128, 128), 0)
    column = lax.broadcasted_iota(jnp.int32, (128, 128), 1)
    group = jnp.where(row >= 80, 2, jnp.where(row >= 40, 1, 0))
    flip = (row + column == 80 * group + 34) & (row < 40 * group + TAPS)
    flip = flip.astype(F32).astype(BF)
    for p, source in enumerate((mine, theirs)):
        block = source[...]
        plain[280 * p : 280 * p + 280, :] = block.astype(F32)
        flipped[280 * p : 280 * p + 280, :] = jnp.dot(block, flip, preferred_element_type=F32)

    def pick(ref, a):
        return jnp.concatenate(
            [ref[8 * a : 8 * a + 8, :], ref[280 + 8 * a : 288 + 8 * a, :]], axis=0
        )

    parts = (pick(plain, 0) + pick(plain, 1)) + pick(plain, 2)
    for i in range(3):
        wgt[16 * i : 16 * i + 16, :] = jnp.broadcast_to(parts[:, 120 + i : 121 + i], (16, 256))
    lane = lax.broadcasted_iota(jnp.int32, (16, 128), 1)
    empty = jnp.zeros((16, 128), BF)
    for i in range(3):
        tiles = [None] * 10
        for a in range(TAPS):
            first, off = divmod(STEP * a, 128)
            turned = pick(flipped, a)
            if (off - SLOT * i) % 128:
                turned = pltpu.roll(turned, (off - SLOT * i) % 128, 1)
            inside = min(STEP, 128 - off)
            piece = jnp.where((lane >= off) & (lane < off + inside), turned, 0.0)
            tiles[first] = piece if tiles[first] is None else tiles[first] + piece
            if inside < STEP:
                piece = jnp.where(lane < STEP - inside, turned, 0.0)
                tiles[first + 1] = piece
        for x in range(BLOCK):
            top = 128 * i + 16 * x
            for n, tile in enumerate(shifted(tiles, STEP * x, 12, lane)):
                fwd[top : top + 16, 128 * n : 128 * n + 128] = (
                    empty if tile is None else tile.astype(BF)
                )
    turned = []
    for q in range(5):
        lines = []
        for e in range(8):
            a = TAPS - 1 - 8 * q - e
            lines.append(pick(plain, a) if a >= 0 else jnp.zeros((16, 128), F32))
        turned.append(jnp.transpose(jnp.concatenate(lines, axis=0)))
    lane = lax.broadcasted_iota(jnp.int32, (SLOT, 128), 1)
    zero = jnp.zeros((SLOT, 128), F32)
    for i in range(3):
        tiles = [t[SLOT * i : SLOT * i + SLOT] for t in turned]
        for x in range(0, BLOCK, 2):
            a = shifted(tiles, 16 * (x + LEAD), 6, lane)
            b = shifted(tiles, 16 * (x + 1 + LEAD), 6, lane)
            for n in range(6):
                both = [zero if t is None else t for t in (a[n], b[n])]
                at = 128 * (3 * n + i)
                adj[SLOT * x : SLOT * (x + 2), at : at + 128] = jnp.concatenate(both, axis=0).astype(BF)


def share(adj, charge, j, count=BLOCK):
    low = max(0, 40 - 8 * j)
    high = min(48, 72 - 8 * j)
    first = low - 40 + 8 * j
    return jnp.dot(
        adj[: SLOT * count, 48 * low : 48 * high],
        charge[48 * first : 48 * (first + high - low), :],
        preferred_element_type=F32,
    )


def fold(part, i):
    moved = pltpu.roll(part[SLOT * i : SLOT * i + SLOT], 0, 1, stride=1, stride_axis=0)
    line = jnp.sum(moved, axis=0, keepdims=True)
    return pltpu.roll(line, WIDE - 34, 1)[:, :256]


def main_body(one, own, two, tgt, wgt, fwd, adj, image_in, res_out, one_out, two_out, some_out, charge,
              image, rows, side, lines, ends, up_out, dn_out):
    del image_in
    even = lax.rem(lax.axis_index("row"), 2) == 0
    below = one[...].astype(F32)
    above = two[...].astype(F32)
    rows[0:17, :] = jnp.where(even, above, below)[15:32]
    rows[17:49, :] = own[...].astype(F32)
    rows[49:66, :] = jnp.where(even, below, above)[0:17]
    rows[66:72, :] = jnp.zeros((6, 512), F32)
    spread(rows, image, 0, 5)
    spread(rows, image, 12, 17)
    spread_ends(rows, side, lines, ends)
    weight = wgt[...].reshape(3, 1, 16, 256)
    target = tgt[...].astype(F32)
    goal = pltpu.roll(target, 512 - 111, 1)[:, :256]
    low = lax.broadcasted_iota(jnp.int32, (8, 128), 1) < 64
    late = lax.broadcasted_iota(jnp.int32, (8, 128), 1) >= 111

    def tail(j):
        return pltpu.roll(target[8 * j : 8 * j + 8, 256:], (64 * (j % 2) - 103) % 256, 1)[:, :128]

    goal_ends = [jnp.where(low, tail(0), tail(1)), jnp.where(low, tail(2), tail(3))]

    def respond(pixels, want):
        fields = jnp.dot(fwd[...], pixels, preferred_element_type=F32)
        fields = fields.reshape(3, BLOCK, 16, 256)
        squares = weight * fields * fields
        intensity = jnp.sum((squares[0] + squares[1]) + squares[2], axis=1)
        resist = jax.nn.sigmoid(STEEP * (intensity - THRESHOLD))
        slope = GAIN * (resist - want) * resist * (1.0 - resist)
        slope = jnp.where(want > 1.5, 0.0, slope)
        scaled = (2.0 * weight) * slope[None, :, None, :] * fields
        return resist, scaled.reshape(384, 256)

    resist_ends, scaled = respond(ends[...], jnp.concatenate(goal_ends, axis=1))
    for j in range(4):
        tile = scaled[:, 128 * (j // 2) : 128 * (j // 2) + 128]
        tile = pltpu.roll(tile, 120 - 64 * (j % 2), 1)
        charge[384 * j : 384 * j + 384, 256:] = tile.astype(BF)
    for j in range(4):
        resist, scaled = respond(image[288 * j : 288 * j + FWD_K, :], goal[8 * j : 8 * j + 8])
        charge[384 * j : 384 * j + 384, :256] = scaled.astype(BF)
        resist = pltpu.roll(resist, 256 - MARGIN, 1)
        end = resist_ends[:, 128 * (j // 2) : 128 * (j // 2) + 128]
        end = pltpu.roll(end, (103 - 64 * (j % 2)) % 128, 1)
        res_out[8 * j : 8 * j + 8, :128] = resist[:, :128]
        res_out[8 * j : 8 * j + 8, 128:] = jnp.where(late, end, resist[:, 128:])
    up_out[0:15, :] = jnp.zeros((15, 256), F32)
    dn_out[17:32, :] = jnp.zeros((15, 256), F32)
    for j, count in ((0, 8), (1, 8), (2, 1), (6, 8), (7, 8), (8, 2)):
        part = share(adj, charge, j, count)
        for i in range(count):
            x = 8 * j + i - MARGIN
            if x < 0:
                up_out[ROWS + x : ROWS + x + 1, :] = fold(part, i)
            elif x < ROWS:
                some_out[...] = jnp.broadcast_to(fold(part, i), (8, 256))
            else:
                dn_out[x - ROWS : x - ROWS + 1, :] = fold(part, i)
    one_out[...] = jnp.where(even, dn_out[...], up_out[...])
    two_out[...] = jnp.where(even, up_out[...], dn_out[...])


def rest_body(adj, charge, some, mid_out):
    mid_out[31:32, :] = some[0:1, :]
    for j in (2, 3, 4, 5):
        part = share(adj, charge, j)
        for i in range(BLOCK):
            x = 8 * j + i - MARGIN
            if x >= 0:
                mid_out[x : x + 1, :] = fold(part, i)


def per_device(mask_levels, level_offset, target_bits, socs_kernels, kernel_weights):
    kern = lax.axis_index("kern")
    col = lax.axis_index("col")
    n_row, n_col = lax.axis_size("row"), lax.axis_size("col")
    left = kern == 0
    wide = lambda dtype: jax.ShapeDtypeStruct((ROWS, 512), dtype)
    strip, mask_full, mask_bf, target, kernels, parts = pl.pallas_call(
        start_body,
        out_shape=(
            pltpu.VMEM((ROWS, 128), BF),
            pltpu.VMEM((ROWS, 512), F32),
            pltpu.VMEM((ROWS, 512), BF),
            pltpu.VMEM((ROWS, 512), BF),
            pltpu.VMEM((12, TAPS, 2, TAPS), BF),
            pltpu.VMEM((24, 128), F32),
        ),
        in_specs=[HBM] * 5,
        out_specs=(VMEM,) * 6,
        scratch_shapes=[
            pltpu.VMEM((ROWS, 512), jnp.int32),
            pltpu.VMEM((ROWS, 512), F32),
            pltpu.VMEM((ROWS, 512), jnp.int32),
            pltpu.SMEM((12,), F32),
            pltpu.SemaphoreType.DMA((5,)),
        ],
        compiler_params=pltpu.CompilerParams(vmem_limit_bytes=START_VMEM),
        name="start",
    )(mask_levels, level_offset, target_bits, jnp.transpose(socs_kernels, (1, 2, 0, 3)), kernel_weights)
    to_right = [(2 * c, 2 * c + 2) for c in range(n_col - 1)]
    to_left = [(2 * c + 3, 2 * c + 1) for c in range(n_col - 1)]
    strip_in = lax.ppermute(strip, ("col", "kern"), to_right + to_left)
    packed = pl.pallas_call(
        pack_body,
        out_shape=jax.ShapeDtypeStruct((280, 128), BF),
        in_specs=[VMEM] * 2,
        out_specs=VMEM,
        scratch_shapes=[pltpu.VMEM((72, 128), F32), pltpu.VMEM((840, 128), F32)],
        compiler_params=pltpu.CompilerParams(vmem_limit_bytes=16 * 2**20),
        cost_estimate=pl.CostEstimate(flops=10**6, bytes_accessed=3 * 10**5, transcendentals=0),
        name="pack",
    )(kernels, parts)
    swap = [(0, 1), (1, 0)]
    other = lax.ppermute(packed, "kern", swap)
    outside = jnp.where(left, col == 0, col == n_col - 1)
    edge_mask = jnp.where(outside, jnp.zeros((), BF), strip_in[:, :64])
    edge_target = jnp.where(outside, jnp.full((), 2.0, BF), strip_in[:, 64:])
    blank = jnp.zeros((ROWS, 64), BF)

    def window(value, edge):
        return jnp.where(
            left,
            jnp.concatenate([blank, edge, value[:, :384]], axis=1),
            jnp.concatenate([value[:, 128:], edge, blank], axis=1),
        )

    own = window(mask_bf, edge_mask)
    goal = window(target, edge_target)
    near = [(i, i ^ 1) for i in range(n_row)]
    far = [(i, ((i + 1) ^ 1) - 1) for i in range(1, n_row - 1)]
    one = lax.ppermute(own, "row", near)
    two = lax.ppermute(own, "row", far)
    image = pl.pallas_call(
        own_body,
        out_shape=jax.ShapeDtypeStruct((IMAGE, 256), BF),
        in_specs=[VMEM],
        out_specs=VMEM,
        scratch_shapes=[pltpu.VMEM((56, 512), F32)],
        compiler_params=pltpu.CompilerParams(vmem_limit_bytes=16 * 2**20),
        cost_estimate=pl.CostEstimate(flops=10**8, bytes_accessed=10**6, transcendentals=0),
        name="own",
    )(own)
    fwd, adj, weights = pl.pallas_call(
        taps_body,
        out_shape=(
            jax.ShapeDtypeStruct((384, FWD_K), BF),
            jax.ShapeDtypeStruct((SLOT * BLOCK, ADJ_K), BF),
            jax.ShapeDtypeStruct((CHANNELS, 256), F32),
        ),
        in_specs=[VMEM] * 2,
        out_specs=(VMEM,) * 3,
        scratch_shapes=[
            pltpu.VMEM((560, 128), F32),
            pltpu.VMEM((560, 128), F32),
        ],
        compiler_params=pltpu.CompilerParams(vmem_limit_bytes=16 * 2**20),
        cost_estimate=pl.CostEstimate(flops=4 * 10**8, bytes_accessed=4 * 10**6, transcendentals=0),
        name="taps",
    )(packed, other)
    tile = jax.ShapeDtypeStruct((ROWS, 256), F32)
    resist, share_one, share_two, some, charge, _ = pl.pallas_call(
        main_body,
        out_shape=(
            tile,
            tile,
            tile,
            jax.ShapeDtypeStruct((8, 256), F32),
            jax.ShapeDtypeStruct((1536, WIDE), BF),
            jax.ShapeDtypeStruct((IMAGE, 256), BF),
        ),
        input_output_aliases={7: 5},
        in_specs=[VMEM] * 8,
        out_specs=(VMEM,) * 6,
        scratch_shapes=[
            pltpu.VMEM((72, 512), F32),
            pltpu.VMEM((72, 128), F32),
            pltpu.VMEM((240, 256), F32),
            pltpu.VMEM((FWD_K, 256), BF),
            pltpu.VMEM((ROWS, 256), F32),
            pltpu.VMEM((ROWS, 256), F32),
        ],
        compiler_params=pltpu.CompilerParams(vmem_limit_bytes=24 * 2**20),
        cost_estimate=pl.CostEstimate(flops=6 * 10**9, bytes_accessed=6 * 10**6, transcendentals=0),
        name="fields",
    )(one, own, two, goal, weights, fwd, adj, image)
    got_two = lax.ppermute(share_two, "row", far)
    got_one = lax.ppermute(share_one, "row", near)
    middle_rows = pl.pallas_call(
        rest_body,
        out_shape=tile,
        in_specs=[VMEM] * 3,
        out_specs=VMEM,
        compiler_params=pltpu.CompilerParams(vmem_limit_bytes=16 * 2**20),
        cost_estimate=pl.CostEstimate(flops=2 * 10**9, bytes_accessed=3 * 10**6, transcendentals=0),
        name="inner",
    )(adj, charge, some)
    half = jnp.where(left, mask_full[:, :256], mask_full[:, 256:])
    gradient = (middle_rows + got_one + got_two) * half * (1.0 - half)
    mine = jnp.concatenate([resist, gradient], axis=0)
    mine = lax.reduce_precision(mine, 8, 7)
    theirs = lax.ppermute(mine.astype(BF), "kern", swap).astype(F32)
    both = jnp.where(
        left, jnp.concatenate([mine, theirs], axis=1), jnp.concatenate([theirs, mine], axis=1)
    )
    return both[:ROWS], both[ROWS:]


def solution(mesh):
    return jax.shard_map(
        per_device,
        mesh=mesh,
        in_specs=(
            P("row", "col"),
            P("row", "col"),
            P("row", "col"),
            P(None, "kern", None, None),
            P("kern"),
        ),
        out_specs=(P("row", "col"), P("row", "col")),
        check_vma=False,
    )
```

```python
import jax
import jax.numpy as jnp
from jax import lax
from jax.experimental import pallas as pl
from jax.experimental.pallas import tpu as pltpu
from jax.sharding import PartitionSpec as P

STEEP = 4.0
THRESHOLD = 1.0
GAIN = 128.0
TAPS = 35
MARGIN = 17
SLOT = 40
STEP = 36
BLOCK = 8
ROWS = 32
CHANNELS = 48
FWD_K = 1536
ADJ_K = 2304
LEAD = 6
WIDE = 384
IMAGE = 17 * 4 * STEP
START_VMEM = 58 * 2**20
BF = jnp.bfloat16
F32 = jnp.float32
VMEM = pl.BlockSpec(memory_space=pltpu.VMEM)
HBM = pl.BlockSpec(memory_space=pltpu.HBM)


def start_body(levels, offset, bits, kernels, weights, strip, full, short, goal, kernels_v, parts,
               levels_v, offset_v, bits_v, weights_v, sems):
    sources = (kernels, weights, levels, offset, bits)
    targets = (kernels_v, weights_v, levels_v, offset_v, bits_v)
    moves = [pltpu.make_async_copy(a, b, sems.at[n]) for n, (a, b) in enumerate(zip(sources, targets))]
    for move in moves:
        move.start()
    left = lax.axis_index("kern") == 0
    for move in moves[2:]:
        move.wait()
    value = jax.nn.sigmoid(2.0 * (levels_v[...].astype(F32) - 1.5) + offset_v[...])
    full[...] = value
    want = bits_v[...].astype(F32)
    short[...] = value.astype(BF)
    goal[...] = want.astype(BF)
    low = lax.broadcasted_iota(jnp.int32, (ROWS, 128), 1) < 64
    ends = jnp.where(low, pltpu.roll(value[:, -128:], 64, 1), want[:, -128:])
    starts = jnp.where(low, value[:, :128], pltpu.roll(want[:, :128], 64, 1))
    strip[...] = jnp.where(left, ends, starts).astype(BF)
    for move in moves[:2]:
        move.wait()
    row = lax.broadcasted_iota(jnp.int32, (8, 128), 0)
    lane = lax.broadcasted_iota(jnp.int32, (8, 128), 1)
    index = 4 * jnp.maximum(lane - 120, 0) + lax.rem(row, 4)
    table = jnp.zeros((8, 128), F32)
    for n in range(12):
        table = jnp.where(index == n, weights_v[n], table)
    table = jnp.where((lane >= 120) & (lane < 123), table, 0.0)
    high = table.astype(BF).astype(F32)
    middle = (table - high).astype(BF).astype(F32)
    lower = table - high - middle
    parts[0:8, :] = high
    parts[8:16, :] = middle
    parts[16:24, :] = lower


def pack_body(kernels, parts, packed, plane, lines):
    plane[...] = jnp.zeros((72, 128), F32)
    for n in range(12):
        plane[0:70, 0:TAPS] = kernels[n].astype(F32).reshape(70, TAPS)
        lines[pl.ds(280 * (n // 4) + n % 4, 70, stride=4), :] = plane[0:70, :]
    lines[0:24, :] = lines[0:24, :] + parts[...]
    tile = lines[0:280, :] + pltpu.roll(lines[280:560, :], 40, 1) + pltpu.roll(lines[560:840, :], 80, 1)
    packed[...] = tile.astype(BF)


def shifted(tiles, shift, count, lane):
    skip, rest = divmod(shift, 128)
    if rest:
        turned = [None if t is None else pltpu.roll(t, rest, 1) for t in tiles]
    else:
        turned = tiles
    get = lambda n: turned[n] if 0 <= n < len(turned) else None
    out = []
    for n in range(count):
        here = get(n - skip)
        if rest:
            before = get(n - skip - 1)
            if here is not None and before is not None:
                here = jnp.where(lane >= rest, here, before)
            elif here is not None:
                here = jnp.where(lane >= rest, here, 0.0)
            elif before is not None:
                here = jnp.where(lane < rest, before, 0.0)
        out.append(here)
    return out


def turn(line, count, shift):
    line = jnp.broadcast_to(line, (count, line.shape[1]))
    return pltpu.roll(line, shift, 1, stride=1, stride_axis=0)


def spread(rows, image, first, last):
    early = lax.broadcasted_iota(jnp.int32, (8, 256), 0) < 4
    for n in range(first, last):
        parts = []
        for r in (4 * n, 4 * n + 2):
            a, b = rows[r : r + 1, :WIDE], rows[r + 1 : r + 2, :WIDE]
            parts.append(turn(a, 32, 0)[:, 128:])
            mixed = pltpu.roll(turn(b, 8, 0)[:, 128:], 4, 0)
            parts.append(jnp.where(early, turn(a, 8, 32)[:, 128:], mixed))
            parts.append(turn(b, 32, 4)[:, 128:])
        image[144 * n : 144 * n + 144, :] = jnp.concatenate(parts, axis=0).astype(BF)


def spread_ends(rows, side, lines, ends):
    low = lax.broadcasted_iota(jnp.int32, (24, 128), 1) < 64
    side[...] = pltpu.roll(rows[:, 256:], 192, 1)[:, :128]
    for e in range(2):
        moved = [side[pl.ds(8 * j + e, 24, stride=2), :] for j in range(4)]
        for n in range(5):
            shift = 8 * n - 4 * e
            for t in range(2):
                one = pltpu.roll(moved[2 * t], (shift - 56) % 128, 1)
                two = pltpu.roll(moved[2 * t + 1], (shift + 8) % 128, 1)
                at = 24 * (5 * e + n)
                lines[at : at + 24, 128 * t : 128 * t + 128] = jnp.where(low, one, two)
    early = lax.broadcasted_iota(jnp.int32, (8, 128), 0) < 4
    for t in range(2):
        lanes = slice(128 * t, 128 * t + 128)
        parts = []
        for c in range(21):
            get = lambda e, n: turn(lines[24 * (5 * e + n) + c : 24 * (5 * e + n) + c + 1, lanes], 8, 0)
            parts += [get(0, n) for n in range(4)]
            parts.append(jnp.where(early, get(0, 4), get(1, 0)))
            parts += [get(1, n) for n in range(1, 5)]
            if c % 2:
                ends[72 * (c - 1) : 72 * (c + 1), lanes] = jnp.concatenate(parts, axis=0).astype(BF)
                parts = []
        parts.append(jnp.zeros((24, 128), F32))
        ends[1440:1536, lanes] = jnp.concatenate(parts, axis=0).astype(BF)


def own_body(own, image, rows):
    rows[17:49, :] = own[...].astype(F32)
    spread(rows, image, 5, 12)


def taps_body(mine, theirs, fwd, adj, wgt, plain, flipped):
    row = lax.broadcasted_iota(jnp.int32, (128, 128), 0)
    column = lax.broadcasted_iota(jnp.int32, (128, 128), 1)
    group = jnp.where(row >= 80, 2, jnp.where(row >= 40, 1, 0))
    flip = (row + column == 80 * group + 34) & (row < 40 * group + TAPS)
    flip = flip.astype(F32).astype(BF)
    for p, source in enumerate((mine, theirs)):
        block = source[...]
        plain[280 * p : 280 * p + 280, :] = block.astype(F32)
        flipped[280 * p : 280 * p + 280, :] = jnp.dot(block, flip, preferred_element_type=F32)

    def pick(ref, a):
        return jnp.concatenate(
            [ref[8 * a : 8 * a + 8, :], ref[280 + 8 * a : 288 + 8 * a, :]], axis=0
        )

    parts = (pick(plain, 0) + pick(plain, 1)) + pick(plain, 2)
    for i in range(3):
        wgt[16 * i : 16 * i + 16, :] = jnp.broadcast_to(parts[:, 120 + i : 121 + i], (16, 256))
    lane = lax.broadcasted_iota(jnp.int32, (16, 128), 1)
    empty = jnp.zeros((16, 128), BF)
    for i in range(3):
        tiles = [None] * 10
        for a in range(TAPS):
            first, off = divmod(STEP * a, 128)
            turned = pick(flipped, a)
            if (off - SLOT * i) % 128:
                turned = pltpu.roll(turned, (off - SLOT * i) % 128, 1)
            inside = min(STEP, 128 - off)
            piece = jnp.where((lane >= off) & (lane < off + inside), turned, 0.0)
            tiles[first] = piece if tiles[first] is None else tiles[first] + piece
            if inside < STEP:
                piece = jnp.where(lane < STEP - inside, turned, 0.0)
                tiles[first + 1] = piece
        for x in range(BLOCK):
            top = 128 * i + 16 * x
            for n, tile in enumerate(shifted(tiles, STEP * x, 12, lane)):
                fwd[top : top + 16, 128 * n : 128 * n + 128] = (
                    empty if tile is None else tile.astype(BF)
                )
    turned = []
    for q in range(5):
        lines = []
        for e in range(8):
            a = TAPS - 1 - 8 * q - e
            lines.append(pick(plain, a) if a >= 0 else jnp.zeros((16, 128), F32))
        turned.append(jnp.transpose(jnp.concatenate(lines, axis=0)))
    lane = lax.broadcasted_iota(jnp.int32, (SLOT, 128), 1)
    zero = jnp.zeros((SLOT, 128), F32)
    for i in range(3):
        tiles = [t[SLOT * i : SLOT * i + SLOT] for t in turned]
        for x in range(0, BLOCK, 2):
            a = shifted(tiles, 16 * (x + LEAD), 6, lane)
            b = shifted(tiles, 16 * (x + 1 + LEAD), 6, lane)
            for n in range(6):
                both = [zero if t is None else t for t in (a[n], b[n])]
                at = 128 * (3 * n + i)
                adj[SLOT * x : SLOT * (x + 2), at : at + 128] = jnp.concatenate(both, axis=0).astype(BF)


def share(adj, charge, j, count=BLOCK):
    low = max(0, 40 - 8 * j)
    high = min(48, 72 - 8 * j)
    first = low - 40 + 8 * j
    return jnp.dot(
        adj[: SLOT * count, 48 * low : 48 * high],
        charge[48 * first : 48 * (first + high - low), :],
        preferred_element_type=F32,
    )


def fold(part, i):
    moved = pltpu.roll(part[SLOT * i : SLOT * i + SLOT], 0, 1, stride=1, stride_axis=0)
    line = jnp.sum(moved, axis=0, keepdims=True)
    return pltpu.roll(line, WIDE - 34, 1)[:, :256]


def main_body(one, own, two, tgt, wgt, fwd, adj, image_in, res_out, one_out, two_out, some_out, charge,
              image, rows, side, lines, ends, up_out, dn_out):
    del image_in
    even = lax.rem(lax.axis_index("row"), 2) == 0
    below = one[...].astype(F32)
    above = two[...].astype(F32)
    rows[0:17, :] = jnp.where(even, above, below)[15:32]
    rows[17:49, :] = own[...].astype(F32)
    rows[49:66, :] = jnp.where(even, below, above)[0:17]
    rows[66:72, :] = jnp.zeros((6, 512), F32)
    spread_ends(rows, side, lines, ends)
    weight = wgt[...].reshape(3, 1, 16, 256)
    target = tgt[...].astype(F32)
    goal = pltpu.roll(target, 512 - 111, 1)[:, :256]
    low = lax.broadcasted_iota(jnp.int32, (8, 128), 1) < 64
    late = lax.broadcasted_iota(jnp.int32, (8, 128), 1) >= 111

    def tail(j):
        return pltpu.roll(target[8 * j : 8 * j + 8, 256:], (64 * (j % 2) - 103) % 256, 1)[:, :128]

    goal_ends = [jnp.where(low, tail(0), tail(1)), jnp.where(low, tail(2), tail(3))]

    def respond(pixels, want):
        fields = jnp.dot(fwd[...], pixels, preferred_element_type=F32)
        fields = fields.reshape(3, BLOCK, 16, 256)
        weighted = weight * fields
        squares = weighted * fields
        intensity = jnp.sum((squares[0] + squares[1]) + squares[2], axis=1)
        resist = jax.nn.sigmoid(STEEP * (intensity - THRESHOLD))
        slope = (2.0 * GAIN) * (resist - want) * resist * (1.0 - resist)
        slope = jnp.where(want > 1.5, 0.0, slope)
        scaled = weighted * slope[None, :, None, :]
        return resist, scaled.reshape(384, 256)

    resist_ends, scaled = respond(ends[...], jnp.concatenate(goal_ends, axis=1))
    spread(rows, image, 0, 5)
    spread(rows, image, 12, 17)
    for j in range(4):
        tile = scaled[:, 128 * (j // 2) : 128 * (j // 2) + 128]
        tile = pltpu.roll(tile, 120 - 64 * (j % 2), 1)
        charge[384 * j : 384 * j + 384, 256:] = tile.astype(BF)
    for j in range(4):
        resist, scaled = respond(image[288 * j : 288 * j + FWD_K, :], goal[8 * j : 8 * j + 8])
        charge[384 * j : 384 * j + 384, :256] = scaled.astype(BF)
        resist = pltpu.roll(resist, 256 - MARGIN, 1)
        end = resist_ends[:, 128 * (j // 2) : 128 * (j // 2) + 128]
        end = pltpu.roll(end, (103 - 64 * (j % 2)) % 128, 1)
        res_out[8 * j : 8 * j + 8, :128] = resist[:, :128]
        res_out[8 * j : 8 * j + 8, 128:] = jnp.where(late, end, resist[:, 128:])
    up_out[0:15, :] = jnp.zeros((15, 256), F32)
    dn_out[17:32, :] = jnp.zeros((15, 256), F32)
    for j, count in ((0, 8), (1, 8), (2, 1), (6, 8), (7, 8), (8, 2)):
        part = share(adj, charge, j, count)
        for i in range(count):
            x = 8 * j + i - MARGIN
            if x < 0:
                up_out[ROWS + x : ROWS + x + 1, :] = fold(part, i)
            elif x < ROWS:
                some_out[...] = jnp.broadcast_to(fold(part, i), (8, 256))
            else:
                dn_out[x - ROWS : x - ROWS + 1, :] = fold(part, i)
    one_out[...] = jnp.where(even, dn_out[...], up_out[...])
    two_out[...] = jnp.where(even, up_out[...], dn_out[...])


def rest_body(adj, charge, some, mid_out):
    mid_out[31:32, :] = some[0:1, :]
    for j in (2, 3, 4, 5):
        part = share(adj, charge, j)
        for i in range(BLOCK):
            x = 8 * j + i - MARGIN
            if x >= 0:
                mid_out[x : x + 1, :] = fold(part, i)


def per_device(mask_levels, level_offset, target_bits, socs_kernels, kernel_weights):
    kern = lax.axis_index("kern")
    col = lax.axis_index("col")
    n_row, n_col = lax.axis_size("row"), lax.axis_size("col")
    left = kern == 0
    wide = lambda dtype: jax.ShapeDtypeStruct((ROWS, 512), dtype)
    strip, mask_full, mask_bf, target, kernels, parts = pl.pallas_call(
        start_body,
        out_shape=(
            pltpu.VMEM((ROWS, 128), BF),
            pltpu.VMEM((ROWS, 512), F32),
            pltpu.VMEM((ROWS, 512), BF),
            pltpu.VMEM((ROWS, 512), BF),
            pltpu.VMEM((12, TAPS, 2, TAPS), BF),
            pltpu.VMEM((24, 128), F32),
        ),
        in_specs=[HBM] * 5,
        out_specs=(VMEM,) * 6,
        scratch_shapes=[
            pltpu.VMEM((ROWS, 512), jnp.int32),
            pltpu.VMEM((ROWS, 512), F32),
            pltpu.VMEM((ROWS, 512), jnp.int32),
            pltpu.SMEM((12,), F32),
            pltpu.SemaphoreType.DMA((5,)),
        ],
        compiler_params=pltpu.CompilerParams(vmem_limit_bytes=START_VMEM),
        name="start",
    )(mask_levels, level_offset, target_bits, jnp.transpose(socs_kernels, (1, 2, 0, 3)), kernel_weights)
    to_right = [(2 * c, 2 * c + 2) for c in range(n_col - 1)]
    to_left = [(2 * c + 3, 2 * c + 1) for c in range(n_col - 1)]
    strip_in = lax.ppermute(strip, ("col", "kern"), to_right + to_left)
    packed = pl.pallas_call(
        pack_body,
        out_shape=jax.ShapeDtypeStruct((280, 128), BF),
        in_specs=[VMEM] * 2,
        out_specs=VMEM,
        scratch_shapes=[pltpu.VMEM((72, 128), F32), pltpu.VMEM((840, 128), F32)],
        compiler_params=pltpu.CompilerParams(vmem_limit_bytes=16 * 2**20),
        cost_estimate=pl.CostEstimate(flops=10**6, bytes_accessed=3 * 10**5, transcendentals=0),
        name="pack",
    )(kernels, parts)
    swap = [(0, 1), (1, 0)]
    other = lax.ppermute(packed, "kern", swap)
    outside = jnp.where(left, col == 0, col == n_col - 1)
    edge_mask = jnp.where(outside, jnp.zeros((), BF), strip_in[:, :64])
    edge_target = jnp.where(outside, jnp.full((), 2.0, BF), strip_in[:, 64:])
    blank = jnp.zeros((ROWS, 64), BF)

    def window(value, edge):
        return jnp.where(
            left,
            jnp.concatenate([blank, edge, value[:, :384]], axis=1),
            jnp.concatenate([value[:, 128:], edge, blank], axis=1),
        )

    own = window(mask_bf, edge_mask)
    goal = window(target, edge_target)
    near = [(i, i ^ 1) for i in range(n_row)]
    far = [(i, ((i + 1) ^ 1) - 1) for i in range(1, n_row - 1)]
    one = lax.ppermute(own, "row", near)
    two = lax.ppermute(own, "row", far)
    image = pl.pallas_call(
        own_body,
        out_shape=jax.ShapeDtypeStruct((IMAGE, 256), BF),
        in_specs=[VMEM],
        out_specs=VMEM,
        scratch_shapes=[pltpu.VMEM((56, 512), F32)],
        compiler_params=pltpu.CompilerParams(vmem_limit_bytes=16 * 2**20),
        cost_estimate=pl.CostEstimate(flops=10**8, bytes_accessed=10**6, transcendentals=0),
        name="own",
    )(own)
    fwd, adj, weights = pl.pallas_call(
        taps_body,
        out_shape=(
            jax.ShapeDtypeStruct((384, FWD_K), BF),
            jax.ShapeDtypeStruct((SLOT * BLOCK, ADJ_K), BF),
            jax.ShapeDtypeStruct((CHANNELS, 256), F32),
        ),
        in_specs=[VMEM] * 2,
        out_specs=(VMEM,) * 3,
        scratch_shapes=[
            pltpu.VMEM((560, 128), F32),
            pltpu.VMEM((560, 128), F32),
        ],
        compiler_params=pltpu.CompilerParams(vmem_limit_bytes=16 * 2**20),
        cost_estimate=pl.CostEstimate(flops=4 * 10**8, bytes_accessed=4 * 10**6, transcendentals=0),
        name="taps",
    )(packed, other)
    tile = jax.ShapeDtypeStruct((ROWS, 256), F32)
    resist, share_one, share_two, some, charge, _ = pl.pallas_call(
        main_body,
        out_shape=(
            tile,
            tile,
            tile,
            jax.ShapeDtypeStruct((8, 256), F32),
            jax.ShapeDtypeStruct((1536, WIDE), BF),
            jax.ShapeDtypeStruct((IMAGE, 256), BF),
        ),
        input_output_aliases={7: 5},
        in_specs=[VMEM] * 8,
        out_specs=(VMEM,) * 6,
        scratch_shapes=[
            pltpu.VMEM((72, 512), F32),
            pltpu.VMEM((72, 128), F32),
            pltpu.VMEM((240, 256), F32),
            pltpu.VMEM((FWD_K, 256), BF),
            pltpu.VMEM((ROWS, 256), F32),
            pltpu.VMEM((ROWS, 256), F32),
        ],
        compiler_params=pltpu.CompilerParams(vmem_limit_bytes=24 * 2**20),
        cost_estimate=pl.CostEstimate(flops=6 * 10**9, bytes_accessed=6 * 10**6, transcendentals=0),
        name="fields",
    )(one, own, two, goal, weights, fwd, adj, image)
    got_two = lax.ppermute(share_two, "row", far)
    got_one = lax.ppermute(share_one, "row", near)
    middle_rows = pl.pallas_call(
        rest_body,
        out_shape=tile,
        in_specs=[VMEM] * 3,
        out_specs=VMEM,
        compiler_params=pltpu.CompilerParams(vmem_limit_bytes=16 * 2**20),
        cost_estimate=pl.CostEstimate(flops=2 * 10**9, bytes_accessed=3 * 10**6, transcendentals=0),
        name="inner",
    )(adj, charge, some)
    half = jnp.where(left, mask_full[:, :256], mask_full[:, 256:])
    gradient = (middle_rows + got_one + got_two) * half * (1.0 - half)
    mine = jnp.concatenate([resist, gradient], axis=0)
    mine = lax.reduce_precision(mine, 8, 7)
    theirs = lax.ppermute(mine.astype(BF), "kern", swap).astype(F32)
    both = jnp.where(
        left, jnp.concatenate([mine, theirs], axis=1), jnp.concatenate([theirs, mine], axis=1)
    )
    return both[:ROWS], both[ROWS:]


def solution(mesh):
    return jax.shard_map(
        per_device,
        mesh=mesh,
        in_specs=(
            P("row", "col"),
            P("row", "col"),
            P("row", "col"),
            P(None, "kern", None, None),
            P("kern"),
        ),
        out_specs=(P("row", "col"), P("row", "col")),
        check_vma=False,
    )
```

```python
import jax
import jax.numpy as jnp
from jax import lax
from jax.experimental import pallas as pl
from jax.experimental.pallas import tpu as pltpu
from jax.sharding import PartitionSpec as P

STEEP = 4.0
THRESHOLD = 1.0
GAIN = 128.0
TAPS = 35
MARGIN = 17
SLOT = 40
STEP = 36
BLOCK = 8
ROWS = 32
CHANNELS = 48
FWD_K = 1536
ADJ_K = 2304
LEAD = 6
WIDE = 384
IMAGE = 17 * 4 * STEP
START_VMEM = 58 * 2**20
BF = jnp.bfloat16
F32 = jnp.float32
VMEM = pl.BlockSpec(memory_space=pltpu.VMEM)
HBM = pl.BlockSpec(memory_space=pltpu.HBM)


def start_body(levels, offset, bits, kernels, weights, strip, full, short, goal, kernels_v, parts,
               levels_v, offset_v, bits_v, weights_v, sems):
    sources = (kernels, weights, levels, offset, bits)
    targets = (kernels_v, weights_v, levels_v, offset_v, bits_v)
    moves = [pltpu.make_async_copy(a, b, sems.at[n]) for n, (a, b) in enumerate(zip(sources, targets))]
    for move in moves:
        move.start()
    left = lax.axis_index("kern") == 0
    for move in moves[2:]:
        move.wait()
    value = jax.nn.sigmoid(2.0 * (levels_v[...].astype(F32) - 1.5) + offset_v[...])
    full[...] = value
    want = bits_v[...].astype(F32)
    short[...] = value.astype(BF)
    goal[...] = want.astype(BF)
    low = lax.broadcasted_iota(jnp.int32, (ROWS, 128), 1) < 64
    ends = jnp.where(low, pltpu.roll(value[:, -128:], 64, 1), want[:, -128:])
    starts = jnp.where(low, value[:, :128], pltpu.roll(want[:, :128], 64, 1))
    strip[...] = jnp.where(left, ends, starts).astype(BF)
    for move in moves[:2]:
        move.wait()
    row = lax.broadcasted_iota(jnp.int32, (8, 128), 0)
    lane = lax.broadcasted_iota(jnp.int32, (8, 128), 1)
    index = 4 * jnp.maximum(lane - 120, 0) + lax.rem(row, 4)
    table = jnp.zeros((8, 128), F32)
    for n in range(12):
        table = jnp.where(index == n, weights_v[n], table)
    table = jnp.where((lane >= 120) & (lane < 123), table, 0.0)
    high = table.astype(BF).astype(F32)
    middle = (table - high).astype(BF).astype(F32)
    lower = table - high - middle
    parts[0:8, :] = high
    parts[8:16, :] = middle
    parts[16:24, :] = lower


def pack_body(kernels, parts, packed, plane, lines):
    plane[...] = jnp.zeros((72, 128), F32)
    for n in range(12):
        plane[0:70, 0:TAPS] = kernels[n].astype(F32).reshape(70, TAPS)
        lines[pl.ds(280 * (n // 4) + n % 4, 70, stride=4), :] = plane[0:70, :]
    lines[0:24, :] = lines[0:24, :] + parts[...]
    tile = lines[0:280, :] + pltpu.roll(lines[280:560, :], 40, 1) + pltpu.roll(lines[560:840, :], 80, 1)
    packed[...] = tile.astype(BF)


def shifted(tiles, shift, count, lane):
    skip, rest = divmod(shift, 128)
    if rest:
        turned = [None if t is None else pltpu.roll(t, rest, 1) for t in tiles]
    else:
        turned = tiles
    get = lambda n: turned[n] if 0 <= n < len(turned) else None
    out = []
    for n in range(count):
        here = get(n - skip)
        if rest:
            before = get(n - skip - 1)
            if here is not None and before is not None:
                here = jnp.where(lane >= rest, here, before)
            elif here is not None:
                here = jnp.where(lane >= rest, here, 0.0)
            elif before is not None:
                here = jnp.where(lane < rest, before, 0.0)
        out.append(here)
    return out


def turn(line, count, shift):
    line = jnp.broadcast_to(line, (count, line.shape[1]))
    return pltpu.roll(line, shift, 1, stride=1, stride_axis=0)


def spread(rows, image, first, last):
    early = lax.broadcasted_iota(jnp.int32, (8, 256), 0) < 4
    for n in range(first, last):
        parts = []
        for r in (4 * n, 4 * n + 2):
            a, b = rows[r : r + 1, :WIDE], rows[r + 1 : r + 2, :WIDE]
            parts.append(turn(a, 32, 0)[:, 128:])
            mixed = pltpu.roll(turn(b, 8, 0)[:, 128:], 4, 0)
            parts.append(jnp.where(early, turn(a, 8, 32)[:, 128:], mixed))
            parts.append(turn(b, 32, 4)[:, 128:])
        image[144 * n : 144 * n + 144, :] = jnp.concatenate(parts, axis=0).astype(BF)


def spread_ends(rows, side, lines, ends):
    low = lax.broadcasted_iota(jnp.int32, (24, 128), 1) < 64
    side[...] = pltpu.roll(rows[:, 256:], 192, 1)[:, :128]
    for e in range(2):
        moved = [side[pl.ds(8 * j + e, 24, stride=2), :] for j in range(4)]
        for n in range(5):
            shift = 8 * n - 4 * e
            for t in range(2):
                one = pltpu.roll(moved[2 * t], (shift - 56) % 128, 1)
                two = pltpu.roll(moved[2 * t + 1], (shift + 8) % 128, 1)
                at = 24 * (5 * e + n)
                lines[at : at + 24, 128 * t : 128 * t + 128] = jnp.where(low, one, two)
    early = lax.broadcasted_iota(jnp.int32, (8, 128), 0) < 4
    for t in range(2):
        lanes = slice(128 * t, 128 * t + 128)
        parts = []
        for c in range(21):
            get = lambda e, n: turn(lines[24 * (5 * e + n) + c : 24 * (5 * e + n) + c + 1, lanes], 8, 0)
            parts += [get(0, n) for n in range(4)]
            parts.append(jnp.where(early, get(0, 4), get(1, 0)))
            parts += [get(1, n) for n in range(1, 5)]
            if c % 2:
                ends[72 * (c - 1) : 72 * (c + 1), lanes] = jnp.concatenate(parts, axis=0).astype(BF)
                parts = []
        parts.append(jnp.zeros((24, 128), F32))
        ends[1440:1536, lanes] = jnp.concatenate(parts, axis=0).astype(BF)


def own_body(own, image, rows):
    rows[17:49, :] = own[...].astype(F32)
    spread(rows, image, 5, 12)


def taps_body(mine, theirs, fwd, adj, wgt, plain, flipped):
    row = lax.broadcasted_iota(jnp.int32, (128, 128), 0)
    column = lax.broadcasted_iota(jnp.int32, (128, 128), 1)
    group = jnp.where(row >= 80, 2, jnp.where(row >= 40, 1, 0))
    flip = (row + column == 80 * group + 34) & (row < 40 * group + TAPS)
    flip = flip.astype(F32).astype(BF)
    for p, source in enumerate((mine, theirs)):
        block = source[...]
        plain[280 * p : 280 * p + 280, :] = block.astype(F32)
        flipped[280 * p : 280 * p + 280, :] = jnp.dot(block, flip, preferred_element_type=F32)

    def pick(ref, a):
        return jnp.concatenate(
            [ref[8 * a : 8 * a + 8, :], ref[280 + 8 * a : 288 + 8 * a, :]], axis=0
        )

    parts = (pick(plain, 0) + pick(plain, 1)) + pick(plain, 2)
    for i in range(3):
        wgt[16 * i : 16 * i + 16, :] = jnp.broadcast_to(parts[:, 120 + i : 121 + i], (16, 256))
    lane = lax.broadcasted_iota(jnp.int32, (16, 128), 1)
    empty = jnp.zeros((16, 128), BF)
    for i in range(3):
        tiles = [None] * 10
        for a in range(TAPS):
            first, off = divmod(STEP * a, 128)
            turned = pick(flipped, a)
            if (off - SLOT * i) % 128:
                turned = pltpu.roll(turned, (off - SLOT * i) % 128, 1)
            inside = min(STEP, 128 - off)
            piece = jnp.where((lane >= off) & (lane < off + inside), turned, 0.0)
            tiles[first] = piece if tiles[first] is None else tiles[first] + piece
            if inside < STEP:
                piece = jnp.where(lane < STEP - inside, turned, 0.0)
                tiles[first + 1] = piece
        for x in range(BLOCK):
            top = 128 * i + 16 * x
            for n, tile in enumerate(shifted(tiles, STEP * x, 12, lane)):
                fwd[top : top + 16, 128 * n : 128 * n + 128] = (
                    empty if tile is None else tile.astype(BF)
                )
    turned = []
    for q in range(5):
        lines = []
        for e in range(8):
            a = TAPS - 1 - 8 * q - e
            lines.append(pick(plain, a) if a >= 0 else jnp.zeros((16, 128), F32))
        turned.append(jnp.transpose(jnp.concatenate(lines, axis=0)))
    lane = lax.broadcasted_iota(jnp.int32, (SLOT, 128), 1)
    zero = jnp.zeros((SLOT, 128), F32)
    for i in range(3):
        tiles = [t[SLOT * i : SLOT * i + SLOT] for t in turned]
        for x in range(0, BLOCK, 2):
            a = shifted(tiles, 16 * (x + LEAD), 6, lane)
            b = shifted(tiles, 16 * (x + 1 + LEAD), 6, lane)
            for n in range(6):
                both = [zero if t is None else t for t in (a[n], b[n])]
                at = 128 * (3 * n + i)
                adj[SLOT * x : SLOT * (x + 2), at : at + 128] = jnp.concatenate(both, axis=0).astype(BF)


def share(adj, charge, j, count=BLOCK):
    low = max(0, 40 - 8 * j)
    high = min(48, 72 - 8 * j)
    first = low - 40 + 8 * j
    return jnp.dot(
        adj[: SLOT * count, 48 * low : 48 * high],
        charge[48 * first : 48 * (first + high - low), :],
        preferred_element_type=F32,
    )


def fold(part, i):
    moved = pltpu.roll(part[SLOT * i : SLOT * i + SLOT], 0, 1, stride=1, stride_axis=0)
    line = jnp.sum(moved, axis=0, keepdims=True)
    return pltpu.roll(line, WIDE - 34, 1)[:, :256]


def main_body(one, own, two, tgt, wgt, fwd, adj, image_in, res_out, one_out, two_out, some_out, charge,
              image, rows, side, lines, ends, up_out, dn_out):
    del image_in
    even = lax.rem(lax.axis_index("row"), 2) == 0
    below = one[...].astype(F32)
    above = two[...].astype(F32)
    rows[0:17, :] = jnp.where(even, above, below)[15:32]
    rows[17:49, :] = own[...].astype(F32)
    rows[49:66, :] = jnp.where(even, below, above)[0:17]
    rows[66:72, :] = jnp.zeros((6, 512), F32)
    spread(rows, image, 0, 5)
    spread(rows, image, 12, 17)
    spread_ends(rows, side, lines, ends)
    weight = wgt[...].reshape(3, 1, 16, 256)
    target = tgt[...].astype(F32)
    goal = pltpu.roll(target, 512 - 111, 1)[:, :256]
    low = lax.broadcasted_iota(jnp.int32, (8, 128), 1) < 64
    late = lax.broadcasted_iota(jnp.int32, (8, 128), 1) >= 111

    def tail(j):
        return pltpu.roll(target[8 * j : 8 * j + 8, 256:], (64 * (j % 2) - 103) % 256, 1)[:, :128]

    goal_ends = [jnp.where(low, tail(0), tail(1)), jnp.where(low, tail(2), tail(3))]

    def respond(pixels, want):
        fields = jnp.dot(fwd[...], pixels, preferred_element_type=F32)
        fields = fields.reshape(3, BLOCK, 16, 256)
        squares = weight * fields * fields
        intensity = jnp.sum((squares[0] + squares[1]) + squares[2], axis=1)
        resist = jax.nn.sigmoid(STEEP * (intensity - THRESHOLD))
        slope = GAIN * (resist - want) * resist * (1.0 - resist)
        slope = jnp.where(want > 1.5, 0.0, slope)
        scaled = (2.0 * weight) * slope[None, :, None, :] * fields
        return resist, scaled.reshape(384, 256)

    resist_ends, scaled = respond(ends[...], jnp.concatenate(goal_ends, axis=1))
    for j in range(4):
        tile = scaled[:, 128 * (j // 2) : 128 * (j // 2) + 128]
        tile = pltpu.roll(tile, 120 - 64 * (j % 2), 1)
        charge[384 * j : 384 * j + 384, 256:] = tile.astype(BF)
    for j in range(4):
        resist, scaled = respond(image[288 * j : 288 * j + FWD_K, :], goal[8 * j : 8 * j + 8])
        charge[384 * j : 384 * j + 384, :256] = scaled.astype(BF)
        resist = pltpu.roll(resist, 256 - MARGIN, 1)
        end = resist_ends[:, 128 * (j // 2) : 128 * (j // 2) + 128]
        end = pltpu.roll(end, (103 - 64 * (j % 2)) % 128, 1)
        res_out[8 * j : 8 * j + 8, :128] = resist[:, :128]
        res_out[8 * j : 8 * j + 8, 128:] = jnp.where(late, end, resist[:, 128:])
    up_out[0:15, :] = jnp.zeros((15, 256), F32)
    dn_out[17:32, :] = jnp.zeros((15, 256), F32)
    for j, count in ((0, 8), (1, 8), (2, 1), (6, 8), (7, 8), (8, 2)):
        part = share(adj, charge, j, count)
        for i in range(count):
            x = 8 * j + i - MARGIN
            if x < 0:
                up_out[ROWS + x : ROWS + x + 1, :] = fold(part, i)
            elif x < ROWS:
                some_out[...] = jnp.broadcast_to(fold(part, i), (8, 256))
            else:
                dn_out[x - ROWS : x - ROWS + 1, :] = fold(part, i)
    one_out[...] = jnp.where(even, dn_out[...], up_out[...]).astype(BF)
    two_out[...] = jnp.where(even, up_out[...], dn_out[...]).astype(BF)


def rest_body(adj, charge, some, mid_out):
    mid_out[31:32, :] = some[0:1, :]
    for j in (2, 3, 4, 5):
        part = share(adj, charge, j)
        for i in range(BLOCK):
            x = 8 * j + i - MARGIN
            if x >= 0:
                mid_out[x : x + 1, :] = fold(part, i)


def per_device(mask_levels, level_offset, target_bits, socs_kernels, kernel_weights):
    kern = lax.axis_index("kern")
    col = lax.axis_index("col")
    n_row, n_col = lax.axis_size("row"), lax.axis_size("col")
    left = kern == 0
    wide = lambda dtype: jax.ShapeDtypeStruct((ROWS, 512), dtype)
    strip, mask_full, mask_bf, target, kernels, parts = pl.pallas_call(
        start_body,
        out_shape=(
            pltpu.VMEM((ROWS, 128), BF),
            pltpu.VMEM((ROWS, 512), F32),
            pltpu.VMEM((ROWS, 512), BF),
            pltpu.VMEM((ROWS, 512), BF),
            pltpu.VMEM((12, TAPS, 2, TAPS), BF),
            pltpu.VMEM((24, 128), F32),
        ),
        in_specs=[HBM] * 5,
        out_specs=(VMEM,) * 6,
        scratch_shapes=[
            pltpu.VMEM((ROWS, 512), jnp.int32),
            pltpu.VMEM((ROWS, 512), F32),
            pltpu.VMEM((ROWS, 512), jnp.int32),
            pltpu.SMEM((12,), F32),
            pltpu.SemaphoreType.DMA((5,)),
        ],
        compiler_params=pltpu.CompilerParams(vmem_limit_bytes=START_VMEM),
        name="start",
    )(mask_levels, level_offset, target_bits, jnp.transpose(socs_kernels, (1, 2, 0, 3)), kernel_weights)
    to_right = [(2 * c, 2 * c + 2) for c in range(n_col - 1)]
    to_left = [(2 * c + 3, 2 * c + 1) for c in range(n_col - 1)]
    strip_in = lax.ppermute(strip, ("col", "kern"), to_right + to_left)
    packed = pl.pallas_call(
        pack_body,
        out_shape=jax.ShapeDtypeStruct((280, 128), BF),
        in_specs=[VMEM] * 2,
        out_specs=VMEM,
        scratch_shapes=[pltpu.VMEM((72, 128), F32), pltpu.VMEM((840, 128), F32)],
        compiler_params=pltpu.CompilerParams(vmem_limit_bytes=16 * 2**20),
        cost_estimate=pl.CostEstimate(flops=10**6, bytes_accessed=3 * 10**5, transcendentals=0),
        name="pack",
    )(kernels, parts)
    swap = [(0, 1), (1, 0)]
    other = lax.ppermute(packed, "kern", swap)
    outside = jnp.where(left, col == 0, col == n_col - 1)
    edge_mask = jnp.where(outside, jnp.zeros((), BF), strip_in[:, :64])
    edge_target = jnp.where(outside, jnp.full((), 2.0, BF), strip_in[:, 64:])
    blank = jnp.zeros((ROWS, 64), BF)

    def window(value, edge):
        return jnp.where(
            left,
            jnp.concatenate([blank, edge, value[:, :384]], axis=1),
            jnp.concatenate([value[:, 128:], edge, blank], axis=1),
        )

    own = window(mask_bf, edge_mask)
    goal = window(target, edge_target)
    near = [(i, i ^ 1) for i in range(n_row)]
    far = [(i, ((i + 1) ^ 1) - 1) for i in range(1, n_row - 1)]
    one = lax.ppermute(own, "row", near)
    two = lax.ppermute(own, "row", far)
    image = pl.pallas_call(
        own_body,
        out_shape=jax.ShapeDtypeStruct((IMAGE, 256), BF),
        in_specs=[VMEM],
        out_specs=VMEM,
        scratch_shapes=[pltpu.VMEM((56, 512), F32)],
        compiler_params=pltpu.CompilerParams(vmem_limit_bytes=16 * 2**20),
        cost_estimate=pl.CostEstimate(flops=10**8, bytes_accessed=10**6, transcendentals=0),
        name="own",
    )(own)
    fwd, adj, weights = pl.pallas_call(
        taps_body,
        out_shape=(
            jax.ShapeDtypeStruct((384, FWD_K), BF),
            jax.ShapeDtypeStruct((SLOT * BLOCK, ADJ_K), BF),
            jax.ShapeDtypeStruct((CHANNELS, 256), F32),
        ),
        in_specs=[VMEM] * 2,
        out_specs=(VMEM,) * 3,
        scratch_shapes=[
            pltpu.VMEM((560, 128), F32),
            pltpu.VMEM((560, 128), F32),
        ],
        compiler_params=pltpu.CompilerParams(vmem_limit_bytes=16 * 2**20),
        cost_estimate=pl.CostEstimate(flops=4 * 10**8, bytes_accessed=4 * 10**6, transcendentals=0),
        name="taps",
    )(packed, other)
    tile = jax.ShapeDtypeStruct((ROWS, 256), F32)
    resist, share_one, share_two, some, charge, _ = pl.pallas_call(
        main_body,
        out_shape=(
            tile,
            jax.ShapeDtypeStruct((ROWS, 256), BF),
            jax.ShapeDtypeStruct((ROWS, 256), BF),
            jax.ShapeDtypeStruct((8, 256), F32),
            jax.ShapeDtypeStruct((1536, WIDE), BF),
            jax.ShapeDtypeStruct((IMAGE, 256), BF),
        ),
        input_output_aliases={7: 5},
        in_specs=[VMEM] * 8,
        out_specs=(VMEM,) * 6,
        scratch_shapes=[
            pltpu.VMEM((72, 512), F32),
            pltpu.VMEM((72, 128), F32),
            pltpu.VMEM((240, 256), F32),
            pltpu.VMEM((FWD_K, 256), BF),
            pltpu.VMEM((ROWS, 256), F32),
            pltpu.VMEM((ROWS, 256), F32),
        ],
        compiler_params=pltpu.CompilerParams(vmem_limit_bytes=24 * 2**20),
        cost_estimate=pl.CostEstimate(flops=6 * 10**9, bytes_accessed=6 * 10**6, transcendentals=0),
        name="fields",
    )(one, own, two, goal, weights, fwd, adj, image)
    got_two = lax.ppermute(share_two, "row", far)
    got_one = lax.ppermute(share_one, "row", near)
    middle_rows = pl.pallas_call(
        rest_body,
        out_shape=tile,
        in_specs=[VMEM] * 3,
        out_specs=VMEM,
        compiler_params=pltpu.CompilerParams(vmem_limit_bytes=16 * 2**20),
        cost_estimate=pl.CostEstimate(flops=2 * 10**9, bytes_accessed=3 * 10**6, transcendentals=0),
        name="inner",
    )(adj, charge, some)
    half = jnp.where(left, mask_full[:, :256], mask_full[:, 256:])
    gradient = (middle_rows + got_one.astype(F32) + got_two.astype(F32)) * half * (1.0 - half)
    mine = jnp.concatenate([resist, gradient], axis=0)
    mine = lax.reduce_precision(mine, 8, 7)
    theirs = lax.ppermute(mine.astype(BF), "kern", swap).astype(F32)
    both = jnp.where(
        left, jnp.concatenate([mine, theirs], axis=1), jnp.concatenate([theirs, mine], axis=1)
    )
    return both[:ROWS], both[ROWS:]


def solution(mesh):
    return jax.shard_map(
        per_device,
        mesh=mesh,
        in_specs=(
            P("row", "col"),
            P("row", "col"),
            P("row", "col"),
            P(None, "kern", None, None),
            P("kern"),
        ),
        out_specs=(P("row", "col"), P("row", "col")),
        check_vma=False,
    )
```
